32 devices in a mesh: dp: 2 (over core), sx: 2 (over x), syz: 8 (over z, y).
Axes of the slice: x: 2, y: 2, z: 4, core: 2. Of those that a mesh axis runs over, the one named last changes fastest.
Arguments:
- volume: bfloat16 [2, 16, 32, 128, 256], P('dp', 'sx', 'syz'), may hold values from -80 to 80
- kernel: bfloat16 [3, 3, 3, 32, 256], replicated, may hold values from -1.36082763 to 1.36082763
Outputs:
- whitened: bfloat16 [2, 16, 32, 128, 256], P('dp', 'sx', 'syz')
The draws below stay inside these ranges and needn't reach their ends.
All inputs are finite; a program needn't handle non-finite values.
Results may differ from the reference program's by a relative error of at most 0.006.
Values may be sent and summed in bfloat16 or wider, within the bound.
A program may use at most 128 MiB of HBM per device.

```python
import jax
import jax.numpy as jnp
from jax import lax

NZ = 128
CHAN = 256
GROUPS = 8
WGROUPS = 2
STEPS = 5
GC = 32
WG = 128
SAMPLES = 2
NX = 16
NY = 32


def draw_volume(key, part):
    keys = jax.random.split(key, 2)
    shape = (SAMPLES, NX, NY, NZ, CHAN)
    places_x = (jnp.arange(NX, dtype=jnp.float32) / NX).reshape(1, NX, 1, 1, 1)
    places_y = (jnp.arange(NY, dtype=jnp.float32) / NY).reshape(1, 1, NY, 1, 1)
    rough = jnp.exp(jax.random.uniform(keys[1], shape, jnp.float32, -0.7, 0.7))
    base = jnp.clip(jax.random.normal(keys[0], shape, jnp.float32), -4.0, 4.0)
    values = base * 10.0 ** (0.5 * (places_x + places_y)) * rough
    return jnp.clip(values, -80.0, 80.0).astype(jnp.bfloat16)


def draw_kernel(key, part):
    keys = jax.random.split(key, 2)
    base = jnp.clip(jax.random.normal(keys[0], (3, 3, 3, GC, CHAN), jnp.float32), -4.0, 4.0)
    column_scale = jnp.exp(jax.random.uniform(keys[1], (1, 1, 1, 1, CHAN), jnp.float32, 0.0, 2.302585))
    return (base * column_scale / (27.0 * GC) ** 0.5).astype(jnp.bfloat16)


def setup_inputs(seed: int = 0) -> dict:
    key_of = jax.random.split(jax.random.key(seed), 3)
    return {
        "volume": draw_volume(jax.random.fold_in(key_of[2], 71), 0),
        "kernel": draw_kernel(jax.random.fold_in(key_of[2], 71), 0),
    }


highest = lax.Precision.HIGHEST
epsilon = 1e-05

def whiten_matrix(covariance):
    identity = jnp.eye(covariance.shape[-1], dtype=jnp.float32)
    shifted = covariance + epsilon * identity
    frobenius = jnp.sqrt(lax.optimization_barrier(jnp.sum(shifted * shifted, axis=(1, 2))))[:, None, None]
    iterate_y = shifted / frobenius
    iterate_z = jnp.broadcast_to(identity, shifted.shape)
    for number in range(STEPS):
        factor = 1.5 * identity - 0.5 * jnp.einsum('gab,gbc->gac', iterate_z, iterate_y, precision=highest)
        iterate_y = jnp.einsum('gab,gbc->gac', iterate_y, factor, precision=highest)
        iterate_z = jnp.einsum('gab,gbc->gac', factor, iterate_z, precision=highest)
    return iterate_z / jnp.sqrt(frobenius)

def convolve(sample, kernel):
    result = lax.conv_general_dilated(sample[None].astype(jnp.float32), kernel.astype(jnp.float32), (1, 1, 1), ((1, 1), (1, 1), (1, 1)), dimension_numbers=('NDHWC', 'DHWIO', 'NDHWC'), feature_group_count=GROUPS, precision=highest)
    return result[0].astype(jnp.bfloat16)

def reference(volume, kernel):
    hidden = lax.map(lambda sample: convolve(sample, kernel), volume)
    voxels = hidden.reshape(-1, WGROUPS, WG)
    counts = float(voxels.shape[0])
    wide_voxels = voxels.astype(jnp.float32)
    sum_first = lax.optimization_barrier(jnp.sum(wide_voxels, axis=0))
    sum_second = jnp.einsum('nga,ngb->gab', wide_voxels, wide_voxels, precision=highest)
    average = sum_first / counts
    covariance = sum_second / counts - average[:, :, None] * average[:, None, :]
    whitener = whiten_matrix(covariance)
    whitener_b = whitener.astype(jnp.bfloat16).astype(jnp.float32)
    shift = lax.optimization_barrier(jnp.sum(whitener_b * average[:, None, :], axis=2))
    result = jnp.einsum('nga,gba->ngb', wide_voxels, whitener_b, precision=highest) - shift
    return result.astype(jnp.bfloat16).reshape(volume.shape)
```

```python
import functools

import jax
import jax.numpy as jnp
from jax import lax
from jax.experimental import pallas as pl
from jax.experimental.pallas import tpu as pltpu
from jax.sharding import PartitionSpec as P

WGROUPS = 2
STEPS = 5
epsilon = 1e-05
highest = lax.Precision.HIGHEST
MESH = pl.DeviceIdType.MESH
F32 = jnp.float32
BF16 = jnp.bfloat16


def fma(a, b):
    return jnp.dot(a, b, preferred_element_type=F32)


def fdot(a, b):
    def halves(m):
        top = m.astype(BF16)
        return top, (m - top.astype(F32)).astype(BF16)

    n = b.shape[1]
    left = jnp.concatenate(halves(a), axis=1)
    right = jnp.concatenate(halves(b), axis=1)
    both = fma(left, jnp.concatenate([right, right], axis=0))
    return both[:, :n] + both[:, n:]


def subsets(stage):
    return [stage] if len(stage) == 1 else [stage[:1], stage[1:], stage]


def main_kernel(
    sizes, stages, parts, whole_count, chunks,
    v_ref, k_ref, hid, white_ref, shift_ref,
    xs, wd, acc, passing, gram, red, got, give, got_pair, fin, got_fin,
    load_sem, send_dir, recv_dir, send_diag, recv_diag, send_pass, recv_pass,
    send_x, recv_x, send_c, recv_c,
    pair_send, pair_recv, tree_send, tree_recv,
):
    nx, ny = sizes
    X, Y, Z, C = v_ref.shape[1:]
    GC = k_ref.shape[1]
    WG = C // WGROUPS
    CH = X // chunks
    me_d = lax.axis_index("dp")
    me_x = lax.axis_index("sx")
    me_y = lax.axis_index("syz")

    def flips(bits):
        where = {}
        for axis, bit in bits:
            me = lax.axis_index(axis)
            where[axis] = where.get(axis, me) + bit - 2 * bit * ((me // bit) % 2)
        return where

    load = pltpu.make_async_copy(
        v_ref.at[0], xs.at[pl.ds(1, X), pl.ds(1, Y), :, pl.ds(C, C)], load_sem)
    load.start()

    odd = me_y % 2
    sign = 2 * odd - 1
    direct, diagonal = me_y - sign, me_y + sign
    behind, ahead = me_y - 2 * sign, me_y + 2 * sign

    def inside(v):
        return (v >= 0) & (v < ny)

    def rerouted(i):
        m = i // 2
        pairs = ny // 2
        return (chunks * jnp.where(i % 2 == 1, pairs - 1 - m, m)) // pairs

    def has_x(d):
        return (me_x + d >= 0) & (me_x + d < nx)

    has_diag = inside(diagonal)
    my_rerouted = jnp.where(has_diag, rerouted(me_y), 0)
    to_pass = jnp.where(inside(behind), rerouted(direct), 0)
    mirrored = (me_x + 1) % 2

    barrier = pltpu.get_barrier_semaphore()

    def greet(where):
        pl.semaphore_signal(barrier, inc=1, device_id=where, device_id_type=MESH)

    greet({"syz": direct})
    greeted = 1
    for ok, where in (
        (has_diag, {"syz": diagonal}),
        (inside(behind), {"syz": behind}),
        (inside(ahead), {"syz": ahead}),
        (has_x(-1), {"sx": me_x - 1}),
        (has_x(1), {"sx": me_x + 1}),
    ):
        @pl.when(ok)
        def _(where=where):
            greet(where)
        greeted += jnp.where(ok, 1, 0)
    pair = flips((("dp", 1),))
    far = [pair] + [flips(bits) for stage in stages for bits in subsets(stage)]
    for who in far:
        greet(who)

    lanes = lax.broadcasted_iota(jnp.int32, (GC, C), 1) // GC

    @pl.loop(0, k_ref.shape[0])
    def _(t):
        w = k_ref[t].astype(F32)
        for g in range(C // GC):
            wd[t, pl.ds(g * GC, GC), :] = jnp.where(lanes == g, w, 0.0).astype(BF16)

    pl.semaphore_wait(barrier, greeted + len(far))

    def plane_of(j):
        return jnp.where(mirrored == 1, X - (j + 1) * CH, j * CH)

    row_direct, row_diag = (Y - 1) * (1 - odd), (Y - 1) * odd
    to_direct, to_diag = (Y + 1) * odd, (Y + 1) * (1 - odd)
    in_direct, in_diag = (Y + 1) * (1 - odd), (Y + 1) * odd

    def middle(px, py):
        return xs.at[px, py, :, pl.ds(C, C)]

    def to_direct_copy(j):
        p = plane_of(j)
        return pltpu.make_async_remote_copy(
            src_ref=v_ref.at[0, pl.ds(p, CH), row_direct],
            dst_ref=middle(pl.ds(p + 1, CH), to_direct),
            send_sem=send_dir.at[j], recv_sem=recv_dir.at[j],
            device_id={"syz": direct}, device_id_type=MESH)

    def to_diag_copy(j):
        p = plane_of(j)
        return pltpu.make_async_remote_copy(
            src_ref=v_ref.at[0, pl.ds(p, CH), row_diag],
            dst_ref=middle(pl.ds(p + 1, CH), to_diag),
            send_sem=send_diag.at[j], recv_sem=recv_diag.at[j],
            device_id={"syz": diagonal}, device_id_type=MESH)

    def detour_copy(j):
        return pltpu.make_async_remote_copy(
            src_ref=v_ref.at[0, pl.ds(plane_of(j), CH), row_diag],
            dst_ref=passing.at[j],
            send_sem=send_diag.at[j], recv_sem=recv_pass.at[j],
            device_id={"syz": direct}, device_id_type=MESH)

    def onward_copy(j):
        return pltpu.make_async_remote_copy(
            src_ref=passing.at[j],
            dst_ref=middle(pl.ds(plane_of(j) + 1, CH), to_direct),
            send_sem=send_pass.at[j], recv_sem=recv_diag.at[j],
            device_id={"syz": behind}, device_id_type=MESH)

    def x_copy(d):
        i = (d + 1) // 2
        return pltpu.make_async_remote_copy(
            src_ref=v_ref.at[0, 0 if d < 0 else X - 1],
            dst_ref=middle(X + 1 if d < 0 else 0, pl.ds(1, Y)),
            send_sem=send_x.at[i], recv_sem=recv_x.at[1 - i],
            device_id={"sx": me_x + d}, device_id_type=MESH)

    def corner_copy(d, side, py):
        i = (d + 1) // 2
        return pltpu.make_async_remote_copy(
            src_ref=middle(1 if d < 0 else X, py),
            dst_ref=middle(X + 1 if d < 0 else 0, py),
            send_sem=send_c.at[i, side], recv_sem=recv_c.at[1 - i, side],
            device_id={"sx": me_x + d}, device_id_type=MESH)

    for j in range(chunks):
        @pl.when(j < my_rerouted)
        def _(j=j):
            detour_copy(j).start()
    for d in (-1, 1):
        @pl.when(has_x(d))
        def _(d=d):
            x_copy(d).start()
    for j in range(chunks):
        to_direct_copy(j).start()

        @pl.when(has_diag & (j >= my_rerouted))
        def _(j=j):
            to_diag_copy(j).start()

    def pass_on(j):
        @pl.when(j < to_pass)
        def _():
            detour_copy(j).wait_recv()
            onward_copy(j).start()

    rows = lax.broadcasted_iota(jnp.int32, (Z, C), 0)

    def shifted(px, py):
        v = xs[px, py, :, pl.ds(C, C)].astype(F32)
        xs[px, py, :, pl.ds(0, C)] = jnp.where(rows == 0, 0.0, pltpu.roll(v, 1, 0)).astype(BF16)
        xs[px, py, :, pl.ds(2 * C, C)] = jnp.where(
            rows == Z - 1, 0.0, pltpu.roll(v, Z - 1, 0)).astype(BF16)

    load.wait()

    @pl.loop(1, X + 1)
    def _(px):
        for py in range(1, Y + 1):
            shifted(px, py)

    def weight(a, b):
        return wd[pl.ds(((a + 1) * 3 + b + 1) * 3, 3)].reshape(3 * C, C)

    def inner(px, y0, n):
        return xs[px, pl.ds(y0, n)].reshape(n * Z, 3 * C)

    def plane(x, offsets, fresh):
        full = sum(fma(inner(x + 1 + a, 1, Y), weight(a, 0)) for a in offsets)
        if fresh:
            acc[x + 1] = full
        else:
            acc[x + 1] += full
        if Y > 1:
            m = (Y - 1) * Z
            acc[x + 1, pl.ds(Z, m)] += sum(fma(inner(x + 1 + a, 1, Y - 1), weight(a, -1)) for a in offsets)
            acc[x + 1, pl.ds(0, m)] += sum(fma(inner(x + 1 + a, 2, Y - 1), weight(a, 1)) for a in offsets)

    if X == 1:
        plane(0, (0,), True)
    else:
        plane(0, (0, 1), True)
        if X > 2:
            @pl.loop(1, X - 1)
            def _(x):
                @pl.when((x >= 2) & (x - 2 < chunks))
                def _():
                    pass_on(x - 2)
                plane(x, (-1, 0, 1), True)
        plane(X - 1, (-1, 0), True)
    for j in range(max(0, X - 3), chunks):
        pass_on(j)

    for d in (-1, 1):
        @pl.when(has_x(d))
        def _(d=d):
            x_copy(-d).wait_recv()
            px = 0 if d < 0 else X + 1
            for py in range(1, Y + 1):
                shifted(px, py)
            plane(0 if d < 0 else X - 1, (d,), False)

    def add_row(px0, n, py, x0, a):
        b = jnp.where(py == 0, 0, 2)
        row = pl.ds(pl.multiple_of(jnp.where(py == 0, 0, Y - 1) * Z, Z), Z)
        lhs = xs[pl.ds(px0, n), py].reshape(n * Z, 3 * C)
        w = wd[pl.ds(((a + 1) * 3 + b) * 3, 3)].reshape(3 * C, C)
        acc[pl.ds(x0 + 1, n), row] += fma(lhs, w).reshape(n, Z, C)

    sides = ((in_direct, True), (in_diag, has_diag))

    def when(ok):
        return (lambda f: f()) if ok is True else pl.when(ok)

    def take(j, p, py):
        for q in range(CH):
            shifted(p + 1 + q, py)
        for a in (-1, 0, 1):
            add_row(p + 1, CH, py, p - a, a)

    def corners_out(d):
        for side, (py, ok) in enumerate(sides):
            @pl.when(has_x(d) if ok is True else has_x(d) & ok)
            def _(side=side, py=py):
                corner_copy(d, side, py).start()

    def corners_in(d, near):
        here = has_x(d) & ((mirrored == (1 if d > 0 else 0)) == near)
        for side, (py, ok) in enumerate(sides):
            @pl.when(here if ok is True else here & ok)
            def _(side=side, py=py):
                corner_copy(-d, side, py).wait_recv()
                px = 0 if d < 0 else X + 1
                shifted(px, py)
                add_row(px, 1, py, 0 if d < 0 else X - 1, d)

    def moments(q):
        x = jnp.where(mirrored == 1, X - 1 - q, q)
        h = acc[x + 1].astype(BF16)
        hid[x] = h
        gram[pl.ds(0, C)] += lax.dot_general(
            h, h, (((0,), (0,)), ((), ())), preferred_element_type=F32)
        gram[pl.ds(C, 8)] += jnp.sum(h.astype(F32).reshape(Y * Z // 8, 8, C), axis=0)

    gram[...] = jnp.zeros_like(gram)
    early = max(0, (chunks - 1) * CH - 1)
    for j in range(chunks):
        p = plane_of(j)
        if j == chunks - 1:
            if chunks > 1:
                for d in (-1, 1):
                    corners_in(d, True)
            if early:
                pl.loop(0, early)(moments)
        to_direct_copy(j).wait_recv()

        @pl.when(has_diag)
        def _(j=j):
            to_diag_copy(j).wait_recv()
        for d in (-1, 1):
            if chunks == 1:
                corners_out(d)
            elif j in (0, chunks - 1):
                @pl.when((mirrored == (1 if d > 0 else 0)) == (j == 0))
                def _(d=d):
                    corners_out(d)
        for py, ok in sides:
            @when(ok)
            def _(j=j, p=p, py=py):
                take(j, p, py)
    for d in (-1, 1):
        if chunks == 1:
            corners_in(d, True)
        corners_in(d, False)
    pl.loop(early, X)(moments)

    mine = me_d == 0
    low = gram[pl.ds(0, WG), pl.ds(0, WG)]
    high = gram[pl.ds(WG, WG), pl.ds(WG, WG)]
    low_sum = gram[pl.ds(C, 8), pl.ds(0, WG)]
    high_sum = gram[pl.ds(C, 8), pl.ds(WG, WG)]
    give[pl.ds(0, WG)] = jnp.where(mine, high, low)
    give[pl.ds(WG, 8)] = jnp.where(mine, high_sum, low_sum)
    swap = pltpu.make_async_remote_copy(
        src_ref=give, dst_ref=got_pair, send_sem=pair_send.at[0], recv_sem=pair_recv.at[0],
        device_id=pair, device_id_type=MESH)
    swap.start()
    own = jnp.where(mine, low, high)
    own_sum = jnp.where(mine, low_sum, high_sum)
    swap.wait()
    red[0, pl.ds(0, WG)] = own + got_pair[pl.ds(0, WG)]
    red[0, pl.ds(WG, 8)] = own_sum + got_pair[pl.ds(WG, 8)]

    count = len(stages)

    def legs(step, stream):
        part = pl.ds(*parts[stream])
        return [
            pltpu.make_async_remote_copy(
                src_ref=red.at[step, part], dst_ref=got.at[step, i, part],
                send_sem=tree_send.at[step, stream, i], recv_sem=tree_recv.at[step, stream, i],
                device_id=flips(bits), device_id_type=MESH)
            for i, bits in enumerate(subsets(stages[(step + stream) % count]))]

    for step in range(count):
        for stream in range(len(parts)):
            for leg in reversed(legs(step, stream)):
                leg.start()
        for stream in range(len(parts)):
            for leg in legs(step, stream):
                leg.wait_recv()
            part = pl.ds(*parts[stream])
            total = red[step, part] + got[step, 0, part]
            if len(stages[(step + stream) % count]) > 1:
                total += got[step, 1, part] + got[step, 2, part]
            red[step + 1, part] = total

    average = jnp.sum(red[count, pl.ds(WG, 8)], axis=0, keepdims=True) / whole_count
    across = jnp.broadcast_to(average, (WG, WG))
    down = across.T
    covariance = red[count, pl.ds(0, WG)] / whole_count - down * across
    identity = jnp.where(
        lax.broadcasted_iota(jnp.int32, (WG, WG), 0) == lax.broadcasted_iota(jnp.int32, (WG, WG), 1),
        1.0, 0.0).astype(F32)
    moved = covariance + epsilon * identity
    square = jnp.sum(jnp.sum(moved * moved, axis=1, keepdims=True), axis=0, keepdims=True)
    frobenius = jnp.sqrt(square)
    y = moved / frobenius
    z = None
    for number in range(STEPS):
        p = 1.5 * identity - 0.5 * (y if z is None else fdot(z, y))
        if number < STEPS - 1:
            y = fdot(y, p)
        z = p if z is None else fdot(p, z)
    whitener = z / jnp.sqrt(frobenius)
    turned = whitener.T.astype(BF16).astype(F32)
    fin[pl.ds(0, WG)] = turned
    fin[pl.ds(WG, 8)] = jnp.broadcast_to(jnp.sum(turned * down, axis=0, keepdims=True), (8, WG))
    swap = pltpu.make_async_remote_copy(
        src_ref=fin, dst_ref=got_fin, send_sem=pair_send.at[1], recv_sem=pair_recv.at[1],
        device_id=pair, device_id_type=MESH)
    swap.start()
    own = fin[...]
    swap.wait()
    other = got_fin[...]
    first = jnp.where(mine, own, other)
    second = jnp.where(mine, other, own)
    white_ref[...] = jnp.zeros_like(white_ref)
    white_ref[pl.ds(0, WG), pl.ds(0, WG)] = first[:WG].astype(BF16)
    white_ref[pl.ds(WG, WG), pl.ds(WG, WG)] = second[:WG].astype(BF16)
    shift_ref[:, pl.ds(0, WG)] = first[WG:]
    shift_ref[:, pl.ds(WG, WG)] = second[WG:]

    for step in range(count):
        for stream in range(len(parts)):
            for leg in legs(step, stream):
                leg.wait_send()
    for j in range(chunks):
        to_direct_copy(j).wait_send()

        @pl.when(has_diag)
        def _(j=j):
            to_diag_copy(j).wait_send()

        @pl.when(j < to_pass)
        def _(j=j):
            onward_copy(j).wait_send()
    for d in (-1, 1):
        @pl.when(has_x(d))
        def _(d=d):
            x_copy(d).wait_send()
        for side, (py, ok) in enumerate(sides):
            @pl.when(has_x(d) if ok is True else has_x(d) & ok)
            def _(d=d, side=side, py=py):
                corner_copy(d, side, py).wait_send()


def apply_kernel(h_ref, w_ref, s_ref, o_ref):
    n = o_ref.shape[0]
    M, C = h_ref.shape[1:]
    h = h_ref[pl.ds(pl.program_id(0) * n, n)]
    result = fma(h.reshape(n * M, C), w_ref[...]) - s_ref[0:1, :]
    o_ref[...] = result.astype(BF16).reshape(o_ref.shape)


def on_device(sizes, volume, kernel):
    nd, nx, ny = sizes
    X, Y, Z, C = volume.shape[1:]
    GC = kernel.shape[3]
    WG = C // WGROUPS
    stages = []
    for axis, n in (("sx", nx), ("syz", ny)):
        bit = 1
        while bit < n:
            stages.append((axis, bit))
            bit *= 2
    stages = [tuple(stages[i:i + 2]) for i in range(0, len(stages), 2)]
    streams = len(stages)
    blocks = (WG + 8) // 8
    edges = [8 * (blocks * i // streams) for i in range(streams + 1)]
    parts = [(edges[i], edges[i + 1] - edges[i]) for i in range(streams)]
    whole_count = float(X * Y * Z * nd * nx * ny)
    R = WG + 8
    count = len(stages)
    dma = pltpu.SemaphoreType.DMA
    chunks = max(n for n in (1, 2, 4) if X % n == 0)
    hidden, white, shift = pl.pallas_call(
        functools.partial(main_kernel, (nx, ny), tuple(stages), tuple(parts), whole_count, chunks),
        out_shape=(
            pltpu.VMEM((X, Y * Z, C), BF16),
            pltpu.VMEM((C, C), BF16),
            pltpu.VMEM((8, C), F32),
        ),
        in_specs=[pl.BlockSpec(memory_space=pl.ANY), pl.BlockSpec(memory_space=pltpu.VMEM)],
        out_specs=(
            pl.BlockSpec(memory_space=pltpu.VMEM),
            pl.BlockSpec(memory_space=pltpu.VMEM),
            pl.BlockSpec(memory_space=pltpu.VMEM),
        ),
        scratch_shapes=[
            pltpu.VMEM((X + 2, Y + 2, Z, 3 * C), BF16),
            pltpu.VMEM((27, C, C), BF16),
            pltpu.VMEM((X + 2, Y * Z, C), F32),
            pltpu.VMEM((chunks, X // chunks, Z, C), BF16),
            pltpu.VMEM((C + 8, C), F32),
            pltpu.VMEM((count + 1, R, WG), F32),
            pltpu.VMEM((count, 3, R, WG), F32),
            pltpu.VMEM((R, WG), F32),
            pltpu.VMEM((R, WG), F32),
            pltpu.VMEM((R, WG), F32),
            pltpu.VMEM((R, WG), F32),
            dma, dma((chunks,)), dma((chunks,)), dma((chunks,)), dma((chunks,)), dma((chunks,)), dma((chunks,)),
            dma((2,)), dma((2,)), dma((2, 2)), dma((2, 2)),
            dma((2,)), dma((2,)), dma((count, streams, 3)), dma((count, streams, 3)),
        ],
        compiler_params=pltpu.CompilerParams(
            collective_id=0, has_side_effects=True, vmem_limit_bytes=56 * 2**20),
        name="conv_moments",
    )(volume, kernel.reshape(27, GC, C))
    result = pl.pallas_call(
        apply_kernel,
        grid=(X // 2,),
        out_shape=jax.ShapeDtypeStruct((X, Y, Z, C), BF16),
        in_specs=[
            pl.BlockSpec(memory_space=pltpu.VMEM),
            pl.BlockSpec(memory_space=pltpu.VMEM),
            pl.BlockSpec(memory_space=pltpu.VMEM),
        ],
        out_specs=pl.BlockSpec((2, Y, Z, C), lambda i: (i, 0, 0, 0)),
        name="apply",
    )(*(pltpu.with_memory_space_constraint(v, pltpu.VMEM) for v in (hidden, white, shift)))
    return result.reshape(volume.shape)


def solution(mesh):
    sizes = (mesh.shape["dp"], mesh.shape["sx"], mesh.shape["syz"])
    placed = (P("dp", "sx", "syz", None, None), P())
    return jax.shard_map(
        functools.partial(on_device, sizes),
        mesh=mesh,
        in_specs=placed,
        out_specs=P("dp", "sx", "syz", None, None),
        check_vma=False,
    )
```

```python
import functools

import jax
import jax.numpy as jnp
from jax import lax
from jax.experimental import pallas as pl
from jax.experimental.pallas import tpu as pltpu
from jax.sharding import PartitionSpec as P

WGROUPS = 2
STEPS = 5
epsilon = 1e-05
highest = lax.Precision.HIGHEST
MESH = pl.DeviceIdType.MESH
F32 = jnp.float32
BF16 = jnp.bfloat16


def fma(a, b):
    return jnp.dot(a, b, preferred_element_type=F32)


def fdot(a, b):
    def halves(m):
        top = m.astype(BF16)
        return top, (m - top.astype(F32)).astype(BF16)

    n = b.shape[1]
    left = jnp.concatenate(halves(a), axis=1)
    right = jnp.concatenate(halves(b), axis=1)
    both = fma(left, jnp.concatenate([right, right], axis=0))
    return both[:, :n] + both[:, n:]


def subsets(stage):
    return [stage] if len(stage) == 1 else [stage[:1], stage[1:], stage]


def main_kernel(
    sizes, stages, parts, whole_count, chunks,
    v_ref, k_ref, hid, white_ref, shift_ref,
    xs, wd, acc, passing, gram, red, got, give, got_pair, fin, got_fin,
    load_sem, send_dir, recv_dir, send_diag, recv_diag, send_pass, recv_pass,
    send_x, recv_x, send_c, recv_c,
    pair_send, pair_recv, tree_send, tree_recv,
):
    nx, ny = sizes
    X, Y, Z, C = v_ref.shape[1:]
    GC = k_ref.shape[1]
    WG = C // WGROUPS
    CH = X // chunks
    me_d = lax.axis_index("dp")
    me_x = lax.axis_index("sx")
    me_y = lax.axis_index("syz")

    def flips(bits):
        where = {}
        for axis, bit in bits:
            me = lax.axis_index(axis)
            where[axis] = where.get(axis, me) + bit - 2 * bit * ((me // bit) % 2)
        return where

    load = pltpu.make_async_copy(
        v_ref.at[0], xs.at[pl.ds(1, X), pl.ds(1, Y), :, pl.ds(C, C)], load_sem)
    load.start()

    odd = me_y % 2
    sign = 2 * odd - 1
    direct, diagonal = me_y - sign, me_y + sign
    behind, ahead = me_y - 2 * sign, me_y + 2 * sign

    def inside(v):
        return (v >= 0) & (v < ny)

    def rerouted(i):
        m = i // 2
        pairs = ny // 2
        return (chunks * jnp.where(i % 2 == 1, pairs - 1 - m, m)) // pairs

    def has_x(d):
        return (me_x + d >= 0) & (me_x + d < nx)

    has_diag = inside(diagonal)
    my_rerouted = jnp.where(has_diag, rerouted(me_y), 0)
    to_pass = jnp.where(inside(behind), rerouted(direct), 0)
    mirrored = (me_x + 1) % 2

    barrier = pltpu.get_barrier_semaphore()

    def greet(where):
        pl.semaphore_signal(barrier, inc=1, device_id=where, device_id_type=MESH)

    pair = flips((("dp", 1),))
    far = [flips(bits) for stage in reversed(stages) for bits in reversed(subsets(stage))] + [pair]
    for who in far:
        greet(who)
    greeted = 0
    other = [(has_x(d) & (me_x % 2 == (0 if d < 0 else 1)), {"sx": me_x + d}) for d in (-1, 1)] if nx > 2 else []
    for ok, where in [
        (has_diag, {"syz": diagonal}),
        (inside(behind), {"syz": behind}),
        (inside(ahead), {"syz": ahead}),
    ] + other:
        @pl.when(ok)
        def _(where=where):
            greet(where)
        greeted += jnp.where(ok, 1, 0)

    lanes = lax.broadcasted_iota(jnp.int32, (GC, C), 1) // GC

    @pl.loop(0, k_ref.shape[0])
    def _(t):
        w = k_ref[t].astype(F32)
        for g in range(C // GC):
            wd[t, pl.ds(g * GC, GC), :] = jnp.where(lanes == g, w, 0.0).astype(BF16)

    pl.semaphore_wait(barrier, greeted + len(far))

    def plane_of(j):
        return jnp.where(mirrored == 1, X - (j + 1) * CH, j * CH)

    row_direct, row_diag = (Y - 1) * (1 - odd), (Y - 1) * odd
    to_direct, to_diag = (Y + 1) * odd, (Y + 1) * (1 - odd)
    in_direct, in_diag = (Y + 1) * (1 - odd), (Y + 1) * odd

    def middle(px, py):
        return xs.at[px, py, :, pl.ds(C, C)]

    def to_direct_copy(j):
        p = plane_of(j)
        return pltpu.make_async_remote_copy(
            src_ref=v_ref.at[0, pl.ds(p, CH), row_direct],
            dst_ref=middle(pl.ds(p + 1, CH), to_direct),
            send_sem=send_dir.at[j], recv_sem=recv_dir.at[j],
            device_id={"syz": direct}, device_id_type=MESH)

    def to_diag_copy(j):
        p = plane_of(j)
        return pltpu.make_async_remote_copy(
            src_ref=v_ref.at[0, pl.ds(p, CH), row_diag],
            dst_ref=middle(pl.ds(p + 1, CH), to_diag),
            send_sem=send_diag.at[j], recv_sem=recv_diag.at[j],
            device_id={"syz": diagonal}, device_id_type=MESH)

    def detour_copy(j):
        return pltpu.make_async_remote_copy(
            src_ref=v_ref.at[0, pl.ds(plane_of(j), CH), row_diag],
            dst_ref=passing.at[j],
            send_sem=send_diag.at[j], recv_sem=recv_pass.at[j],
            device_id={"syz": direct}, device_id_type=MESH)

    def onward_copy(j):
        return pltpu.make_async_remote_copy(
            src_ref=passing.at[j],
            dst_ref=middle(pl.ds(plane_of(j) + 1, CH), to_direct),
            send_sem=send_pass.at[j], recv_sem=recv_diag.at[j],
            device_id={"syz": behind}, device_id_type=MESH)

    def x_copy(d):
        i = (d + 1) // 2
        return pltpu.make_async_remote_copy(
            src_ref=v_ref.at[0, 0 if d < 0 else X - 1],
            dst_ref=middle(X + 1 if d < 0 else 0, pl.ds(1, Y)),
            send_sem=send_x.at[i], recv_sem=recv_x.at[1 - i],
            device_id={"sx": me_x + d}, device_id_type=MESH)

    def corner_copy(d, side, py):
        i = (d + 1) // 2
        return pltpu.make_async_remote_copy(
            src_ref=middle(1 if d < 0 else X, py),
            dst_ref=middle(X + 1 if d < 0 else 0, py),
            send_sem=send_c.at[i, side], recv_sem=recv_c.at[1 - i, side],
            device_id={"sx": me_x + d}, device_id_type=MESH)

    for j in range(chunks):
        @pl.when(j < my_rerouted)
        def _(j=j):
            detour_copy(j).start()
    for d in (-1, 1):
        @pl.when(has_x(d))
        def _(d=d):
            x_copy(d).start()
    def send(j):
        to_direct_copy(j).start()

        @pl.when(has_diag & (j >= my_rerouted))
        def _():
            to_diag_copy(j).start()

    for j in range(chunks if X < 8 else 1):
        send(j)

    def pass_on(j):
        @pl.when(j < to_pass)
        def _():
            detour_copy(j).wait_recv()
            onward_copy(j).start()

    rows = lax.broadcasted_iota(jnp.int32, (Z, C), 0)

    def shifted(px, py):
        v = xs[px, py, :, pl.ds(C, C)].astype(F32)
        xs[px, py, :, pl.ds(0, C)] = jnp.where(rows == 0, 0.0, pltpu.roll(v, 1, 0)).astype(BF16)
        xs[px, py, :, pl.ds(2 * C, C)] = jnp.where(
            rows == Z - 1, 0.0, pltpu.roll(v, Z - 1, 0)).astype(BF16)

    load.wait()

    @pl.loop(1, X + 1)
    def _(px):
        for py in range(1, Y + 1):
            shifted(px, py)

    def weight(a, b):
        return wd[pl.ds(((a + 1) * 3 + b + 1) * 3, 3)].reshape(3 * C, C)

    def inner(px, y0, n):
        return xs[px, pl.ds(y0, n)].reshape(n * Z, 3 * C)

    def plane(x, offsets, fresh):
        full = sum(fma(inner(x + 1 + a, 1, Y), weight(a, 0)) for a in offsets)
        if fresh:
            acc[x + 1] = full
        else:
            acc[x + 1] += full
        if Y > 1:
            m = (Y - 1) * Z
            acc[x + 1, pl.ds(Z, m)] += sum(fma(inner(x + 1 + a, 1, Y - 1), weight(a, -1)) for a in offsets)
            acc[x + 1, pl.ds(0, m)] += sum(fma(inner(x + 1 + a, 2, Y - 1), weight(a, 1)) for a in offsets)

    sides = ((in_direct, True), (in_diag, has_diag))

    def when(ok):
        return (lambda f: f()) if ok is True else pl.when(ok)

    def corners_out(d):
        for side, (py, ok) in enumerate(sides):
            @pl.when(has_x(d) if ok is True else has_x(d) & ok)
            def _(side=side, py=py):
                corner_copy(d, side, py).start()

    def arrived(j):
        to_direct_copy(j).wait_recv()

        @pl.when(has_diag)
        def _():
            to_diag_copy(j).wait_recv()
        for d in (-1, 1):
            if chunks == 1:
                corners_out(d)
            elif j in (0, chunks - 1):
                @pl.when((mirrored == (1 if d > 0 else 0)) == (j == 0))
                def _(d=d):
                    corners_out(d)

    if X == 1:
        plane(0, (0,), True)
    else:
        plane(0, (0, 1), True)
        if X > 2:
            @pl.loop(1, X - 1)
            def _(x):
                @pl.when(x < chunks)
                def _():
                    send(x)
                @pl.when((x >= 3) & (x - 3 < chunks))
                def _():
                    pass_on(x - 3)
                plane(x, (-1, 0, 1), True)

                @pl.when(x == max(1, X - 2))
                def _():
                    arrived(0)
        plane(X - 1, (-1, 0), True)
    for j in range(max(0, X - 3), chunks):
        pass_on(j)
    if X <= 2:
        arrived(0)

    for d in (-1, 1):
        @pl.when(has_x(d))
        def _(d=d):
            x_copy(-d).wait_recv()
            px = 0 if d < 0 else X + 1
            for py in range(1, Y + 1):
                shifted(px, py)
            plane(0 if d < 0 else X - 1, (d,), False)

    def add_row(px0, n, py, x0, a):
        b = jnp.where(py == 0, 0, 2)
        row = pl.ds(pl.multiple_of(jnp.where(py == 0, 0, Y - 1) * Z, Z), Z)
        lhs = xs[pl.ds(px0, n), py].reshape(n * Z, 3 * C)
        w = wd[pl.ds(((a + 1) * 3 + b) * 3, 3)].reshape(3 * C, C)
        acc[pl.ds(x0 + 1, n), row] += fma(lhs, w).reshape(n, Z, C)

    def take(j, p, py):
        for q in range(CH):
            shifted(p + 1 + q, py)
        for a in (-1, 0, 1):
            add_row(p + 1, CH, py, p - a, a)

    def corners_in(d, near):
        here = has_x(d) & ((mirrored == (1 if d > 0 else 0)) == near)
        for side, (py, ok) in enumerate(sides):
            @pl.when(here if ok is True else here & ok)
            def _(side=side, py=py):
                corner_copy(-d, side, py).wait_recv()
                px = 0 if d < 0 else X + 1
                shifted(px, py)
                add_row(px, 1, py, 0 if d < 0 else X - 1, d)

    def moments(q):
        x = jnp.where(mirrored == 1, X - 1 - q, q)
        h = acc[x + 1].astype(BF16)
        hid[x] = h
        gram[pl.ds(0, C)] += lax.dot_general(
            h, h, (((0,), (0,)), ((), ())), preferred_element_type=F32)
        gram[pl.ds(C, 8)] += jnp.sum(h.astype(F32).reshape(Y * Z // 8, 8, C), axis=0)

    gram[...] = jnp.zeros_like(gram)
    early = max(0, (chunks - 1) * CH - 1)
    sooner = max(0, (chunks - 2) * CH - 1)
    for j in range(chunks):
        p = plane_of(j)
        if j == chunks - 1:
            if chunks > 1 and not sooner:
                for d in (-1, 1):
                    corners_in(d, True)
            if early:
                pl.loop(sooner, early)(moments)
        if j and j == chunks - 2 and sooner:
            for d in (-1, 1):
                corners_in(d, True)
            pl.loop(0, sooner)(moments)
        if j:
            arrived(j)
        for py, ok in sides:
            @when(ok)
            def _(j=j, p=p, py=py):
                take(j, p, py)
    for d in (-1, 1):
        if chunks == 1:
            corners_in(d, True)
        corners_in(d, False)
    pl.loop(early, X)(moments)

    mine = me_d == 0
    H = WG // 2
    half = lax.broadcasted_iota(jnp.int32, (H // 2, WG), 1) < H

    def packed(g):
        at = pl.ds(g * WG, WG)
        tail = gram[pl.ds(g * WG + H, H), at]
        return gram[pl.ds(g * WG, H), at], jnp.where(half, pltpu.roll(tail[:H // 2], H, 1), tail[H // 2:]), gram[pl.ds(C, 8), at]

    places = (pl.ds(0, H), pl.ds(H, H // 2), pl.ds(H + H // 2, 8))
    low, high = packed(0), packed(1)
    for place, a, b in zip(places, low, high):
        give[place] = jnp.where(mine, b, a)
    swap = pltpu.make_async_remote_copy(
        src_ref=give, dst_ref=got_pair, send_sem=pair_send.at[0], recv_sem=pair_recv.at[0],
        device_id=pair, device_id_type=MESH)
    swap.start()
    for place, a, b in zip(places, low, high):
        red[0, place] = jnp.where(mine, a, b)
    swap.wait()
    red[0] += got_pair[...]

    count = len(stages)

    def legs(step, stream):
        part = pl.ds(*parts[stream])
        return [
            pltpu.make_async_remote_copy(
                src_ref=red.at[step, part], dst_ref=got.at[step, i, part],
                send_sem=tree_send.at[step, stream, i], recv_sem=tree_recv.at[step, stream, i],
                device_id=flips(bits), device_id_type=MESH)
            for i, bits in enumerate(subsets(stages[(step + stream) % count]))]

    for step in range(count):
        for stream in range(len(parts)):
            for leg in reversed(legs(step, stream)):
                leg.start()
        for stream in range(len(parts)):
            for leg in legs(step, stream):
                leg.wait_recv()
            part = pl.ds(*parts[stream])
            total = red[step, part] + got[step, 0, part]
            if len(stages[(step + stream) % count]) > 1:
                total += got[step, 1, part] + got[step, 2, part]
            red[step + 1, part] = total

    average = jnp.sum(red[count, places[2]], axis=0, keepdims=True) / whole_count
    across = jnp.broadcast_to(average, (WG, WG))
    down = across.T
    top, tail = red[count, places[0]], red[count, places[1]]
    right = jnp.concatenate([top, pltpu.roll(tail, H, 1), tail], axis=0)
    left = lax.broadcasted_iota(jnp.int32, (WG, WG), 1) < H
    lower = lax.broadcasted_iota(jnp.int32, (WG, WG), 0) >= H
    moment = jnp.where(left & lower, right.T, right)
    covariance = moment / whole_count - down * across
    identity = jnp.where(
        lax.broadcasted_iota(jnp.int32, (WG, WG), 0) == lax.broadcasted_iota(jnp.int32, (WG, WG), 1),
        1.0, 0.0).astype(F32)
    moved = covariance + epsilon * identity
    square = jnp.sum(jnp.sum(moved * moved, axis=1, keepdims=True), axis=0, keepdims=True)
    frobenius = jnp.sqrt(square)
    y = moved / frobenius
    z = None
    for number in range(STEPS):
        p = 1.5 * identity - 0.5 * (y if z is None else fdot(z, y))
        if number < STEPS - 1:
            y = fdot(y, p)
        z = p if z is None else fdot(p, z)
    whitener = z / jnp.sqrt(frobenius)
    turned = whitener.astype(BF16).astype(F32)
    fin[pl.ds(0, WG)] = turned
    fin[pl.ds(WG, 8)] = jnp.broadcast_to(jnp.sum(turned * down, axis=0, keepdims=True), (8, WG))
    swap = pltpu.make_async_remote_copy(
        src_ref=fin, dst_ref=got_fin, send_sem=pair_send.at[1], recv_sem=pair_recv.at[1],
        device_id=pair, device_id_type=MESH)
    swap.start()
    own = fin[...]
    swap.wait()
    other = got_fin[...]
    first = jnp.where(mine, own, other)
    second = jnp.where(mine, other, own)
    white_ref[...] = jnp.zeros_like(white_ref)
    white_ref[pl.ds(0, WG), pl.ds(0, WG)] = first[:WG].astype(BF16)
    white_ref[pl.ds(WG, WG), pl.ds(WG, WG)] = second[:WG].astype(BF16)
    shift_ref[:, pl.ds(0, WG)] = first[WG:]
    shift_ref[:, pl.ds(WG, WG)] = second[WG:]

    for step in range(count):
        for stream in range(len(parts)):
            for leg in legs(step, stream):
                leg.wait_send()
    for j in range(chunks):
        to_direct_copy(j).wait_send()

        @pl.when(has_diag)
        def _(j=j):
            to_diag_copy(j).wait_send()

        @pl.when(j < to_pass)
        def _(j=j):
            onward_copy(j).wait_send()
    for d in (-1, 1):
        @pl.when(has_x(d))
        def _(d=d):
            x_copy(d).wait_send()
        for side, (py, ok) in enumerate(sides):
            @pl.when(has_x(d) if ok is True else has_x(d) & ok)
            def _(d=d, side=side, py=py):
                corner_copy(d, side, py).wait_send()


def apply_kernel(h_ref, w_ref, s_ref, o_ref, block, sems):
    X = h_ref.shape[0]
    copies = [pltpu.make_async_copy(block.at[x], o_ref.at[x], sems.at[x]) for x in range(X)]
    for x in range(X):
        result = fma(h_ref[x], w_ref[...]) - s_ref[0:1, :]
        block[x] = result.astype(BF16).reshape(block.shape[1:])
        copies[x].start()
    for copy in copies:
        copy.wait()


def on_device(sizes, volume, kernel):
    nd, nx, ny = sizes
    X, Y, Z, C = volume.shape[1:]
    GC = kernel.shape[3]
    WG = C // WGROUPS
    stages = []
    for axis, n in (("sx", nx), ("syz", ny)):
        bit = 1
        while bit < n:
            stages.append((axis, bit))
            bit *= 2
    stages = [tuple(stages[i:i + 2]) for i in range(0, len(stages), 2)]
    streams = len(stages)
    blocks = (3 * WG // 4 + 8) // 8
    edges = [8 * (blocks * i // streams) for i in range(streams + 1)]
    parts = [(edges[i], edges[i + 1] - edges[i]) for i in range(streams)]
    whole_count = float(X * Y * Z * nd * nx * ny)
    R = 3 * WG // 4 + 8
    count = len(stages)
    dma = pltpu.SemaphoreType.DMA
    chunks = max(n for n in (1, 2, 4) if X % n == 0)
    hidden, white, shift = pl.pallas_call(
        functools.partial(main_kernel, (nx, ny), tuple(stages), tuple(parts), whole_count, chunks),
        out_shape=(
            pltpu.VMEM((X, Y * Z, C), BF16),
            pltpu.VMEM((C, C), BF16),
            pltpu.VMEM((8, C), F32),
        ),
        in_specs=[pl.BlockSpec(memory_space=pl.ANY), pl.BlockSpec(memory_space=pltpu.VMEM)],
        out_specs=(
            pl.BlockSpec(memory_space=pltpu.VMEM),
            pl.BlockSpec(memory_space=pltpu.VMEM),
            pl.BlockSpec(memory_space=pltpu.VMEM),
        ),
        scratch_shapes=[
            pltpu.VMEM((X + 2, Y + 2, Z, 3 * C), BF16),
            pltpu.VMEM((27, C, C), BF16),
            pltpu.VMEM((X + 2, Y * Z, C), F32),
            pltpu.VMEM((chunks, X // chunks, Z, C), BF16),
            pltpu.VMEM((C + 8, C), F32),
            pltpu.VMEM((count + 1, R, WG), F32),
            pltpu.VMEM((count, 3, R, WG), F32),
            pltpu.VMEM((R, WG), F32),
            pltpu.VMEM((R, WG), F32),
            pltpu.VMEM((WG + 8, WG), F32),
            pltpu.VMEM((WG + 8, WG), F32),
            dma, dma((chunks,)), dma((chunks,)), dma((chunks,)), dma((chunks,)), dma((chunks,)), dma((chunks,)),
            dma((2,)), dma((2,)), dma((2, 2)), dma((2, 2)),
            dma((2,)), dma((2,)), dma((count, streams, 3)), dma((count, streams, 3)),
        ],
        compiler_params=pltpu.CompilerParams(
            collective_id=0, has_side_effects=True, vmem_limit_bytes=56 * 2**20),
        name="conv_moments",
    )(volume, kernel.reshape(27, GC, C))
    result = pl.pallas_call(
        apply_kernel,
        out_shape=jax.ShapeDtypeStruct((X, Y, Z, C), BF16),
        in_specs=[pl.BlockSpec(memory_space=pltpu.VMEM)] * 3,
        out_specs=pl.BlockSpec(memory_space=pl.ANY),
        scratch_shapes=[pltpu.VMEM((X, Y, Z, C), BF16), dma((X,))],
        name="apply",
    )(*(pltpu.with_memory_space_constraint(v, pltpu.VMEM) for v in (hidden, white, shift)))
    return result.reshape(volume.shape)


def solution(mesh):
    sizes = (mesh.shape["dp"], mesh.shape["sx"], mesh.shape["syz"])
    placed = (P("dp", "sx", "syz", None, None), P())
    return jax.shard_map(
        functools.partial(on_device, sizes),
        mesh=mesh,
        in_specs=placed,
        out_specs=P("dp", "sx", "syz", None, None),
        check_vma=False,
    )
```

```python
import functools

import jax
import jax.numpy as jnp
from jax import lax
from jax.experimental import pallas as pl
from jax.experimental.pallas import tpu as pltpu
from jax.sharding import PartitionSpec as P

WGROUPS = 2
STEPS = 5
epsilon = 1e-05
highest = lax.Precision.HIGHEST
MESH = pl.DeviceIdType.MESH
F32 = jnp.float32
BF16 = jnp.bfloat16


def fma(a, b):
    return jnp.dot(a, b, preferred_element_type=F32)


def fdot(a, b):
    def halves(m):
        top = m.astype(BF16)
        return top, (m - top.astype(F32)).astype(BF16)

    n = b.shape[1]
    left = jnp.concatenate(halves(a), axis=1)
    right = jnp.concatenate(halves(b), axis=1)
    both = fma(left, jnp.concatenate([right, right], axis=0))
    return both[:, :n] + both[:, n:]


def subsets(stage):
    return [stage] if len(stage) == 1 else [stage[:1], stage[1:], stage]


def main_kernel(
    sizes, stages, parts, whole_count, chunks,
    v_ref, k_ref, hid, white_ref, shift_ref,
    xs, wd, acc, passing, gram, red, got, give, got_pair, fin, got_fin,
    load_sem, send_dir, recv_dir, send_diag, recv_diag, send_pass, recv_pass,
    send_x, recv_x, send_c, recv_c,
    pair_send, pair_recv, tree_send, tree_recv,
):
    nx, ny = sizes
    X, Y, Z, C = v_ref.shape[1:]
    GC = k_ref.shape[1]
    WG = C // WGROUPS
    CH = X // chunks
    me_d = lax.axis_index("dp")
    me_x = lax.axis_index("sx")
    me_y = lax.axis_index("syz")

    def flips(bits):
        where = {}
        for axis, bit in bits:
            me = lax.axis_index(axis)
            where[axis] = where.get(axis, me) + bit - 2 * bit * ((me // bit) % 2)
        return where

    load = pltpu.make_async_copy(
        v_ref.at[0], xs.at[pl.ds(1, X), pl.ds(1, Y), :, pl.ds(C, C)], load_sem)
    load.start()

    odd = me_y % 2
    sign = 2 * odd - 1
    direct, diagonal = me_y - sign, me_y + sign
    behind, ahead = me_y - 2 * sign, me_y + 2 * sign

    def inside(v):
        return (v >= 0) & (v < ny)

    def rerouted(i):
        m = i // 2
        pairs = ny // 2
        return (chunks * jnp.where(i % 2 == 1, pairs - 1 - m, m)) // pairs

    def has_x(d):
        return (me_x + d >= 0) & (me_x + d < nx)

    has_diag = inside(diagonal)
    my_rerouted = jnp.where(has_diag, rerouted(me_y), 0)
    to_pass = jnp.where(inside(behind), rerouted(direct), 0)
    mirrored = (me_x + 1) % 2

    barrier = pltpu.get_barrier_semaphore()

    def greet(where):
        pl.semaphore_signal(barrier, inc=1, device_id=where, device_id_type=MESH)

    pair = flips((("dp", 1),))
    far = [flips(bits) for stage in reversed(stages) for bits in reversed(subsets(stage))] + [pair]
    for who in far:
        greet(who)
    greeted = 0
    other = [(has_x(d) & (me_x % 2 == (0 if d < 0 else 1)), {"sx": me_x + d}) for d in (-1, 1)] if nx > 2 else []
    for ok, where in [
        (has_diag, {"syz": diagonal}),
        (inside(behind), {"syz": behind}),
        (inside(ahead), {"syz": ahead}),
    ] + other:
        @pl.when(ok)
        def _(where=where):
            greet(where)
        greeted += jnp.where(ok, 1, 0)

    lanes = lax.broadcasted_iota(jnp.int32, (GC, C), 1) // GC

    @pl.loop(0, k_ref.shape[0])
    def _(t):
        w = k_ref[t].astype(F32)
        for g in range(C // GC):
            wd[t, pl.ds(g * GC, GC), :] = jnp.where(lanes == g, w, 0.0).astype(BF16)

    pl.semaphore_wait(barrier, greeted + len(far))

    def plane_of(j):
        return jnp.where(mirrored == 1, X - (j + 1) * CH, j * CH)

    row_direct, row_diag = (Y - 1) * (1 - odd), (Y - 1) * odd
    to_direct, to_diag = (Y + 1) * odd, (Y + 1) * (1 - odd)
    in_direct, in_diag = (Y + 1) * (1 - odd), (Y + 1) * odd

    def middle(px, py):
        return xs.at[px, py, :, pl.ds(C, C)]

    def to_direct_copy(j):
        p = plane_of(j)
        return pltpu.make_async_remote_copy(
            src_ref=v_ref.at[0, pl.ds(p, CH), row_direct],
            dst_ref=middle(pl.ds(p + 1, CH), to_direct),
            send_sem=send_dir.at[j], recv_sem=recv_dir.at[j],
            device_id={"syz": direct}, device_id_type=MESH)

    def to_diag_copy(j):
        p = plane_of(j)
        return pltpu.make_async_remote_copy(
            src_ref=v_ref.at[0, pl.ds(p, CH), row_diag],
            dst_ref=middle(pl.ds(p + 1, CH), to_diag),
            send_sem=send_diag.at[j], recv_sem=recv_diag.at[j],
            device_id={"syz": diagonal}, device_id_type=MESH)

    def detour_copy(j):
        return pltpu.make_async_remote_copy(
            src_ref=v_ref.at[0, pl.ds(plane_of(j), CH), row_diag],
            dst_ref=passing.at[j],
            send_sem=send_diag.at[j], recv_sem=recv_pass.at[j],
            device_id={"syz": direct}, device_id_type=MESH)

    def onward_copy(j):
        return pltpu.make_async_remote_copy(
            src_ref=passing.at[j],
            dst_ref=middle(pl.ds(plane_of(j) + 1, CH), to_direct),
            send_sem=send_pass.at[j], recv_sem=recv_diag.at[j],
            device_id={"syz": behind}, device_id_type=MESH)

    def x_copy(d):
        i = (d + 1) // 2
        return pltpu.make_async_remote_copy(
            src_ref=v_ref.at[0, 0 if d < 0 else X - 1],
            dst_ref=middle(X + 1 if d < 0 else 0, pl.ds(1, Y)),
            send_sem=send_x.at[i], recv_sem=recv_x.at[1 - i],
            device_id={"sx": me_x + d}, device_id_type=MESH)

    def corner_copy(d, side, py):
        i = (d + 1) // 2
        return pltpu.make_async_remote_copy(
            src_ref=middle(1 if d < 0 else X, py),
            dst_ref=middle(X + 1 if d < 0 else 0, py),
            send_sem=send_c.at[i, side], recv_sem=recv_c.at[1 - i, side],
            device_id={"sx": me_x + d}, device_id_type=MESH)

    for j in range(chunks):
        @pl.when(j < my_rerouted)
        def _(j=j):
            detour_copy(j).start()
    for d in (-1, 1):
        @pl.when(has_x(d))
        def _(d=d):
            x_copy(d).start()
    def send(j):
        to_direct_copy(j).start()

        @pl.when(has_diag & (j >= my_rerouted))
        def _():
            to_diag_copy(j).start()

    for j in range(chunks if X < 8 else 1):
        send(j)

    def pass_on(j):
        @pl.when(j < to_pass)
        def _():
            detour_copy(j).wait_recv()
            onward_copy(j).start()

    rows = lax.broadcasted_iota(jnp.int32, (Z, C), 0)

    def shifted(px, py):
        v = xs[px, py, :, pl.ds(C, C)].astype(F32)
        xs[px, py, :, pl.ds(0, C)] = jnp.where(rows == 0, 0.0, pltpu.roll(v, 1, 0)).astype(BF16)
        xs[px, py, :, pl.ds(2 * C, C)] = jnp.where(
            rows == Z - 1, 0.0, pltpu.roll(v, Z - 1, 0)).astype(BF16)

    load.wait()

    @pl.loop(1, X + 1)
    def _(px):
        for py in range(1, Y + 1):
            shifted(px, py)

    def weight(a, b):
        return wd[pl.ds(((a + 1) * 3 + b + 1) * 3, 3)].reshape(3 * C, C)

    def inner(px, y0, n):
        return xs[px, pl.ds(y0, n)].reshape(n * Z, 3 * C)

    def plane(x, offsets, fresh):
        full = sum(fma(inner(x + 1 + a, 1, Y), weight(a, 0)) for a in offsets)
        if fresh:
            acc[x + 1] = full
        else:
            acc[x + 1] += full
        if Y > 1:
            m = (Y - 1) * Z
            acc[x + 1, pl.ds(Z, m)] += sum(fma(inner(x + 1 + a, 1, Y - 1), weight(a, -1)) for a in offsets)
            acc[x + 1, pl.ds(0, m)] += sum(fma(inner(x + 1 + a, 2, Y - 1), weight(a, 1)) for a in offsets)

    sides = ((in_direct, True), (in_diag, has_diag))

    def when(ok):
        return (lambda f: f()) if ok is True else pl.when(ok)

    def corners_out(d):
        for side, (py, ok) in enumerate(sides):
            @pl.when(has_x(d) if ok is True else has_x(d) & ok)
            def _(side=side, py=py):
                corner_copy(d, side, py).start()

    def arrived(j):
        to_direct_copy(j).wait_recv()

        @pl.when(has_diag)
        def _():
            to_diag_copy(j).wait_recv()
        for d in (-1, 1):
            if chunks == 1:
                corners_out(d)
            elif j in (0, chunks - 1):
                @pl.when((mirrored == (1 if d > 0 else 0)) == (j == 0))
                def _(d=d):
                    corners_out(d)

    if X == 1:
        plane(0, (0,), True)
    else:
        plane(0, (0, 1), True)
        if X > 2:
            @pl.loop(1, X - 1)
            def _(x):
                @pl.when(x < chunks)
                def _():
                    send(x)
                @pl.when((x >= 3) & (x - 3 < chunks))
                def _():
                    pass_on(x - 3)
                plane(x, (-1, 0, 1), True)

                @pl.when(x == max(1, X - 2))
                def _():
                    arrived(0)
        plane(X - 1, (-1, 0), True)
    for j in range(max(0, X - 3), chunks):
        pass_on(j)
    if X <= 2:
        arrived(0)

    for d in (-1, 1):
        @pl.when(has_x(d))
        def _(d=d):
            x_copy(-d).wait_recv()
            px = 0 if d < 0 else X + 1
            for py in range(1, Y + 1):
                shifted(px, py)
            plane(0 if d < 0 else X - 1, (d,), False)

    def add_row(px0, n, py, x0, a):
        b = jnp.where(py == 0, 0, 2)
        row = pl.ds(pl.multiple_of(jnp.where(py == 0, 0, Y - 1) * Z, Z), Z)
        lhs = xs[pl.ds(px0, n), py].reshape(n * Z, 3 * C)
        w = wd[pl.ds(((a + 1) * 3 + b) * 3, 3)].reshape(3 * C, C)
        acc[pl.ds(x0 + 1, n), row] += fma(lhs, w).reshape(n, Z, C)

    def take(j, p, py):
        for q in range(CH):
            shifted(p + 1 + q, py)
        for a in (-1, 0, 1):
            add_row(p + 1, CH, py, p - a, a)

    def corners_in(d, near):
        here = has_x(d) & ((mirrored == (1 if d > 0 else 0)) == near)
        for side, (py, ok) in enumerate(sides):
            @pl.when(here if ok is True else here & ok)
            def _(side=side, py=py):
                corner_copy(-d, side, py).wait_recv()
                px = 0 if d < 0 else X + 1
                shifted(px, py)
                add_row(px, 1, py, 0 if d < 0 else X - 1, d)

    def moments(q):
        x = jnp.where(mirrored == 1, X - 1 - q, q)
        h = acc[x + 1].astype(BF16)
        hid[x] = h
        gram[pl.ds(0, C)] += lax.dot_general(
            h, h, (((0,), (0,)), ((), ())), preferred_element_type=F32)
        gram[pl.ds(C, 8)] += jnp.sum(h.astype(F32).reshape(Y * Z // 8, 8, C), axis=0)

    gram[...] = jnp.zeros_like(gram)
    early = max(0, (chunks - 1) * CH - 1)
    sooner = max(0, (chunks - 2) * CH - 1)
    for j in range(chunks):
        p = plane_of(j)
        if j == chunks - 1:
            if chunks > 1 and not sooner:
                for d in (-1, 1):
                    corners_in(d, True)
            if early:
                pl.loop(sooner, early)(moments)
        if j and j == chunks - 2 and sooner:
            for d in (-1, 1):
                corners_in(d, True)
            pl.loop(0, sooner)(moments)
        if j:
            arrived(j)
        for py, ok in sides:
            @when(ok)
            def _(j=j, p=p, py=py):
                take(j, p, py)
    for d in (-1, 1):
        if chunks == 1:
            corners_in(d, True)
        corners_in(d, False)
    pl.loop(early, X)(moments)

    mine = me_d == 0
    H = WG // 2
    half = lax.broadcasted_iota(jnp.int32, (H // 2, WG), 1) < H

    def packed(g):
        at = pl.ds(g * WG, WG)
        tail = gram[pl.ds(g * WG + H, H), at]
        return gram[pl.ds(g * WG, H), at], jnp.where(half, pltpu.roll(tail[:H // 2], H, 1), tail[H // 2:]), gram[pl.ds(C, 8), at]

    places = (pl.ds(0, H), pl.ds(H, H // 2), pl.ds(H + H // 2, 8))
    low, high = packed(0), packed(1)
    for place, a, b in zip(places, low, high):
        give[place] = jnp.where(mine, b, a)
    swap = pltpu.make_async_remote_copy(
        src_ref=give, dst_ref=got_pair, send_sem=pair_send.at[0], recv_sem=pair_recv.at[0],
        device_id=pair, device_id_type=MESH)
    swap.start()
    for place, a, b in zip(places, low, high):
        red[0, place] = jnp.where(mine, a, b)
    swap.wait()
    red[0] += got_pair[...]

    count = len(stages)

    def legs(step, stream):
        part = pl.ds(*parts[stream])
        return [
            pltpu.make_async_remote_copy(
                src_ref=red.at[step, part], dst_ref=got.at[step, i, part],
                send_sem=tree_send.at[step, stream, i], recv_sem=tree_recv.at[step, stream, i],
                device_id=flips(bits), device_id_type=MESH)
            for i, bits in enumerate(subsets(stages[(step + stream) % count]))]

    def send_sums(step, stream):
        for leg in reversed(legs(step, stream)):
            leg.start()

    for stream in range(len(parts)):
        send_sums(0, stream)
    for step in range(count):
        for stream in range(len(parts)):
            for leg in legs(step, stream):
                leg.wait_recv()
            part = pl.ds(*parts[stream])
            total = red[step, part] + got[step, 0, part]
            if len(stages[(step + stream) % count]) > 1:
                total += got[step, 1, part] + got[step, 2, part]
            red[step + 1, part] = total
            if step + 1 < count:
                send_sums(step + 1, stream)

    average = jnp.sum(red[count, places[2]], axis=0, keepdims=True) / whole_count
    across = jnp.broadcast_to(average, (WG, WG))
    down = across.T
    top, tail = red[count, places[0]], red[count, places[1]]
    right = jnp.concatenate([top, pltpu.roll(tail, H, 1), tail], axis=0)
    left = lax.broadcasted_iota(jnp.int32, (WG, WG), 1) < H
    lower = lax.broadcasted_iota(jnp.int32, (WG, WG), 0) >= H
    moment = jnp.where(left & lower, right.T, right)
    covariance = moment / whole_count - down * across
    identity = jnp.where(
        lax.broadcasted_iota(jnp.int32, (WG, WG), 0) == lax.broadcasted_iota(jnp.int32, (WG, WG), 1),
        1.0, 0.0).astype(F32)
    moved = covariance + epsilon * identity
    square = jnp.sum(jnp.sum(moved * moved, axis=1, keepdims=True), axis=0, keepdims=True)
    frobenius = jnp.sqrt(square)
    y = moved / frobenius
    z = None
    for number in range(STEPS):
        p = 1.5 * identity - 0.5 * (y if z is None else fdot(z, y))
        if number < STEPS - 1:
            y = fdot(y, p)
        z = p if z is None else fdot(p, z)
    whitener = z / jnp.sqrt(frobenius)
    turned = whitener.astype(BF16).astype(F32)
    fin[pl.ds(0, WG)] = turned
    fin[pl.ds(WG, 8)] = jnp.broadcast_to(jnp.sum(turned * down, axis=0, keepdims=True), (8, WG))
    swap = pltpu.make_async_remote_copy(
        src_ref=fin, dst_ref=got_fin, send_sem=pair_send.at[1], recv_sem=pair_recv.at[1],
        device_id=pair, device_id_type=MESH)
    swap.start()
    own = fin[...]
    swap.wait()
    other = got_fin[...]
    first = jnp.where(mine, own, other)
    second = jnp.where(mine, other, own)
    white_ref[...] = jnp.zeros_like(white_ref)
    white_ref[pl.ds(0, WG), pl.ds(0, WG)] = first[:WG].astype(BF16)
    white_ref[pl.ds(WG, WG), pl.ds(WG, WG)] = second[:WG].astype(BF16)
    shift_ref[:, pl.ds(0, WG)] = first[WG:]
    shift_ref[:, pl.ds(WG, WG)] = second[WG:]

    for step in range(count):
        for stream in range(len(parts)):
            for leg in legs(step, stream):
                leg.wait_send()
    for j in range(chunks):
        to_direct_copy(j).wait_send()

        @pl.when(has_diag)
        def _(j=j):
            to_diag_copy(j).wait_send()

        @pl.when(j < to_pass)
        def _(j=j):
            onward_copy(j).wait_send()
    for d in (-1, 1):
        @pl.when(has_x(d))
        def _(d=d):
            x_copy(d).wait_send()
        for side, (py, ok) in enumerate(sides):
            @pl.when(has_x(d) if ok is True else has_x(d) & ok)
            def _(d=d, side=side, py=py):
                corner_copy(d, side, py).wait_send()


def apply_kernel(h_ref, w_ref, s_ref, o_ref, block, sems):
    X = h_ref.shape[0]
    copies = [pltpu.make_async_copy(block.at[x], o_ref.at[x], sems.at[x]) for x in range(X)]
    for x in range(X):
        result = fma(h_ref[x], w_ref[...]) - s_ref[0:1, :]
        block[x] = result.astype(BF16).reshape(block.shape[1:])
        copies[x].start()
    for copy in copies:
        copy.wait()


def on_device(sizes, volume, kernel):
    nd, nx, ny = sizes
    X, Y, Z, C = volume.shape[1:]
    GC = kernel.shape[3]
    WG = C // WGROUPS
    stages = []
    for axis, n in (("sx", nx), ("syz", ny)):
        bit = 1
        while bit < n:
            stages.append((axis, bit))
            bit *= 2
    stages = [tuple(stages[i:i + 2]) for i in range(0, len(stages), 2)]
    streams = len(stages)
    blocks = (3 * WG // 4 + 8) // 8
    edges = [8 * (blocks * i // streams) for i in range(streams + 1)]
    parts = [(edges[i], edges[i + 1] - edges[i]) for i in range(streams)]
    whole_count = float(X * Y * Z * nd * nx * ny)
    R = 3 * WG // 4 + 8
    count = len(stages)
    dma = pltpu.SemaphoreType.DMA
    chunks = max(n for n in (1, 2, 4) if X % n == 0)
    hidden, white, shift = pl.pallas_call(
        functools.partial(main_kernel, (nx, ny), tuple(stages), tuple(parts), whole_count, chunks),
        out_shape=(
            pltpu.VMEM((X, Y * Z, C), BF16),
            pltpu.VMEM((C, C), BF16),
            pltpu.VMEM((8, C), F32),
        ),
        in_specs=[pl.BlockSpec(memory_space=pl.ANY), pl.BlockSpec(memory_space=pltpu.VMEM)],
        out_specs=(
            pl.BlockSpec(memory_space=pltpu.VMEM),
            pl.BlockSpec(memory_space=pltpu.VMEM),
            pl.BlockSpec(memory_space=pltpu.VMEM),
        ),
        scratch_shapes=[
            pltpu.VMEM((X + 2, Y + 2, Z, 3 * C), BF16),
            pltpu.VMEM((27, C, C), BF16),
            pltpu.VMEM((X + 2, Y * Z, C), F32),
            pltpu.VMEM((chunks, X // chunks, Z, C), BF16),
            pltpu.VMEM((C + 8, C), F32),
            pltpu.VMEM((count + 1, R, WG), F32),
            pltpu.VMEM((count, 3, R, WG), F32),
            pltpu.VMEM((R, WG), F32),
            pltpu.VMEM((R, WG), F32),
            pltpu.VMEM((WG + 8, WG), F32),
            pltpu.VMEM((WG + 8, WG), F32),
            dma, dma((chunks,)), dma((chunks,)), dma((chunks,)), dma((chunks,)), dma((chunks,)), dma((chunks,)),
            dma((2,)), dma((2,)), dma((2, 2)), dma((2, 2)),
            dma((2,)), dma((2,)), dma((count, streams, 3)), dma((count, streams, 3)),
        ],
        compiler_params=pltpu.CompilerParams(
            collective_id=0, has_side_effects=True, vmem_limit_bytes=56 * 2**20),
        name="conv_moments",
    )(volume, kernel.reshape(27, GC, C))
    result = pl.pallas_call(
        apply_kernel,
        out_shape=jax.ShapeDtypeStruct((X, Y, Z, C), BF16),
        in_specs=[pl.BlockSpec(memory_space=pltpu.VMEM)] * 3,
        out_specs=pl.BlockSpec(memory_space=pl.ANY),
        scratch_shapes=[pltpu.VMEM((X, Y, Z, C), BF16), dma((X,))],
        name="apply",
    )(*(pltpu.with_memory_space_constraint(v, pltpu.VMEM) for v in (hidden, white, shift)))
    return result.reshape(volume.shape)


def solution(mesh):
    sizes = (mesh.shape["dp"], mesh.shape["sx"], mesh.shape["syz"])
    placed = (P("dp", "sx", "syz", None, None), P())
    return jax.shard_map(
        functools.partial(on_device, sizes),
        mesh=mesh,
        in_specs=placed,
        out_specs=P("dp", "sx", "syz", None, None),
        check_vma=False,
    )
```

```python
import functools

import jax
import jax.numpy as jnp
from jax import lax
from jax.experimental import pallas as pl
from jax.experimental.pallas import tpu as pltpu
from jax.sharding import PartitionSpec as P

WGROUPS = 2
STEPS = 5
epsilon = 1e-05
highest = lax.Precision.HIGHEST
MESH = pl.DeviceIdType.MESH
F32 = jnp.float32
BF16 = jnp.bfloat16


def fma(a, b):
    return jnp.dot(a, b, preferred_element_type=F32)


def fdot(a, b):
    def halves(m):
        top = m.astype(BF16)
        return top, (m - top.astype(F32)).astype(BF16)

    n = b.shape[1]
    left = jnp.concatenate(halves(a), axis=1)
    right = jnp.concatenate(halves(b), axis=1)
    both = fma(left, jnp.concatenate([right, right], axis=0))
    return both[:, :n] + both[:, n:]


def subsets(stage):
    return [stage] if len(stage) == 1 else [stage[:1], stage[1:], stage]


def main_kernel(
    sizes, stages, parts, whole_count, chunks,
    v_ref, k_ref, hid, white_ref, shift_ref,
    xs, wd, wt, acc, passing, gram, sums, red, got, give, got_pair, fin, got_fin,
    load_sem, send_dir, recv_dir, send_diag, recv_diag, send_pass, recv_pass,
    send_x, recv_x, send_c, recv_c,
    pair_send, pair_recv, tree_send, tree_recv,
):
    nx, ny = sizes
    X, Y, Z, C = v_ref.shape[1:]
    GC = k_ref.shape[1]
    WG = C // WGROUPS
    CH = X // chunks
    me_d = lax.axis_index("dp")
    me_x = lax.axis_index("sx")
    me_y = lax.axis_index("syz")

    def flips(bits):
        where = {}
        for axis, bit in bits:
            me = lax.axis_index(axis)
            where[axis] = where.get(axis, me) + bit - 2 * bit * ((me // bit) % 2)
        return where

    load = pltpu.make_async_copy(
        v_ref.at[0], xs.at[pl.ds(1, X), pl.ds(1, Y), :, pl.ds(C, C)], load_sem)
    load.start()

    odd = me_y % 2
    sign = 2 * odd - 1
    direct, diagonal = me_y - sign, me_y + sign
    behind, ahead = me_y - 2 * sign, me_y + 2 * sign

    def inside(v):
        return (v >= 0) & (v < ny)

    def rerouted(i):
        m = i // 2
        pairs = ny // 2
        return (chunks * jnp.where(i % 2 == 1, pairs - 1 - m, m)) // pairs

    def has_x(d):
        return (me_x + d >= 0) & (me_x + d < nx)

    has_diag = inside(diagonal)
    my_rerouted = jnp.where(has_diag, rerouted(me_y), 0)
    to_pass = jnp.where(inside(behind), rerouted(direct), 0)
    mirrored = (me_x + 1) % 2

    barrier = pltpu.get_barrier_semaphore()

    def greet(where):
        pl.semaphore_signal(barrier, inc=1, device_id=where, device_id_type=MESH)

    pair = flips((("dp", 1),))
    far = [flips(bits) for stage in reversed(stages) for bits in reversed(subsets(stage))] + [pair]
    for who in far:
        greet(who)
    greeted = 0
    other = [(has_x(d) & (me_x % 2 == (0 if d < 0 else 1)), {"sx": me_x + d}) for d in (-1, 1)] if nx > 2 else []
    for ok, where in [
        (has_diag, {"syz": diagonal}),
        (inside(behind), {"syz": behind}),
        (inside(ahead), {"syz": ahead}),
    ] + other:
        @pl.when(ok)
        def _(where=where):
            greet(where)
        greeted += jnp.where(ok, 1, 0)

    lanes = lax.broadcasted_iota(jnp.int32, (GC, C), 1) // GC
    wt[:, :, 0, :, pl.ds(WG, WG)] = jnp.zeros((WGROUPS, 3, 3 * WG, WG), BF16)
    wt[:, :, 3, :, pl.ds(0, WG)] = jnp.zeros((WGROUPS, 3, 3 * WG, WG), BF16)

    @pl.loop(0, k_ref.shape[0])
    def _(t):
        w = k_ref[t].astype(F32)
        for g in range(C // GC):
            masked = jnp.where(lanes == g, w, 0.0).astype(BF16)
            wd[t, pl.ds(g * GC, GC), :] = masked
            h = g * GC // WG
            at = pl.ds(pl.multiple_of((t % 3) * WG + g * GC - h * WG, GC), GC)
            part = masked[:, h * WG:(h + 1) * WG]
            wt[h, t // 9, (t // 3) % 3, at, pl.ds(0, WG)] = part
            wt[h, t // 9, (t // 3) % 3 + 1, at, pl.ds(WG, WG)] = part

    pl.semaphore_wait(barrier, greeted + len(far))

    def plane_of(j):
        return jnp.where(mirrored == 1, X - (j + 1) * CH, j * CH)

    row_direct, row_diag = (Y - 1) * (1 - odd), (Y - 1) * odd
    to_direct, to_diag = (Y + 1) * odd, (Y + 1) * (1 - odd)
    in_direct, in_diag = (Y + 1) * (1 - odd), (Y + 1) * odd

    def middle(px, py):
        return xs.at[px, py, :, pl.ds(C, C)]

    def to_direct_copy(j):
        p = plane_of(j)
        return pltpu.make_async_remote_copy(
            src_ref=v_ref.at[0, pl.ds(p, CH), row_direct],
            dst_ref=middle(pl.ds(p + 1, CH), to_direct),
            send_sem=send_dir.at[j], recv_sem=recv_dir.at[j],
            device_id={"syz": direct}, device_id_type=MESH)

    def to_diag_copy(j):
        p = plane_of(j)
        return pltpu.make_async_remote_copy(
            src_ref=v_ref.at[0, pl.ds(p, CH), row_diag],
            dst_ref=middle(pl.ds(p + 1, CH), to_diag),
            send_sem=send_diag.at[j], recv_sem=recv_diag.at[j],
            device_id={"syz": diagonal}, device_id_type=MESH)

    def detour_copy(j):
        return pltpu.make_async_remote_copy(
            src_ref=v_ref.at[0, pl.ds(plane_of(j), CH), row_diag],
            dst_ref=passing.at[j],
            send_sem=send_diag.at[j], recv_sem=recv_pass.at[j],
            device_id={"syz": direct}, device_id_type=MESH)

    def onward_copy(j):
        return pltpu.make_async_remote_copy(
            src_ref=passing.at[j],
            dst_ref=middle(pl.ds(plane_of(j) + 1, CH), to_direct),
            send_sem=send_pass.at[j], recv_sem=recv_diag.at[j],
            device_id={"syz": behind}, device_id_type=MESH)

    def x_copy(d):
        i = (d + 1) // 2
        return pltpu.make_async_remote_copy(
            src_ref=v_ref.at[0, 0 if d < 0 else X - 1],
            dst_ref=middle(X + 1 if d < 0 else 0, pl.ds(1, Y)),
            send_sem=send_x.at[i], recv_sem=recv_x.at[1 - i],
            device_id={"sx": me_x + d}, device_id_type=MESH)

    def corner_copy(d, side, py):
        i = (d + 1) // 2
        return pltpu.make_async_remote_copy(
            src_ref=middle(1 if d < 0 else X, py),
            dst_ref=middle(X + 1 if d < 0 else 0, py),
            send_sem=send_c.at[i, side], recv_sem=recv_c.at[1 - i, side],
            device_id={"sx": me_x + d}, device_id_type=MESH)

    for j in range(chunks):
        @pl.when(j < my_rerouted)
        def _(j=j):
            detour_copy(j).start()
    for d in (-1, 1):
        @pl.when(has_x(d))
        def _(d=d):
            x_copy(d).start()
    def send(j):
        to_direct_copy(j).start()

        @pl.when(has_diag & (j >= my_rerouted))
        def _():
            to_diag_copy(j).start()

    send(0)

    def pass_on(j):
        @pl.when(j < to_pass)
        def _():
            detour_copy(j).wait_recv()
            onward_copy(j).start()

    rows = lax.broadcasted_iota(jnp.int32, (Z, C), 0)

    def shifted(px, py):
        v = xs[px, py, :, pl.ds(C, C)].astype(F32)
        xs[px, py, :, pl.ds(0, C)] = jnp.where(rows == 0, 0.0, pltpu.roll(v, 1, 0)).astype(BF16)
        xs[px, py, :, pl.ds(2 * C, C)] = jnp.where(
            rows == Z - 1, 0.0, pltpu.roll(v, Z - 1, 0)).astype(BF16)

    load.wait()

    @pl.loop(1, X + 1)
    def _(px):
        for py in range(1, Y + 1):
            shifted(px, py)

    def planes(x, n, offsets, h, fresh):
        for t in range(Y // 2):
            rows = [p for p in range(2 * t - 1, 2 * t + 3) if 0 <= p < Y]
            low = rows[0] - (2 * t - 1)
            def operand(a):
                return [xs[pl.ds(x + 1 + a, n), p + 1, :, pl.ds(c * C + h * WG, WG)].reshape(n * Z, WG)
                        for p in rows for c in range(3)]

            def factor(a):
                return wt[h, a + 1, pl.ds(low, len(rows))].reshape(len(rows) * 3 * WG, 2 * WG)

            both = fma(
                jnp.concatenate([v for a in offsets for v in operand(a)], axis=1),
                jnp.concatenate([factor(a) for a in offsets], axis=0))
            for u in range(2):
                at = (pl.ds(x + 1, n), pl.ds((2 * t + u) * Z, Z), pl.ds(h * WG, WG))
                value = both[:, u * WG:(u + 1) * WG].reshape(n, Z, WG)
                if fresh:
                    acc[at] = value
                else:
                    acc[at] += value

    sides = ((in_direct, True), (in_diag, has_diag))

    def when(ok):
        return (lambda f: f()) if ok is True else pl.when(ok)

    def corners_out(d):
        for side, (py, ok) in enumerate(sides):
            @pl.when(has_x(d) if ok is True else has_x(d) & ok)
            def _(side=side, py=py):
                corner_copy(d, side, py).start()

    def arrived(j):
        to_direct_copy(j).wait_recv()

        @pl.when(has_diag)
        def _():
            to_diag_copy(j).wait_recv()
        for d in (-1, 1):
            if chunks == 1:
                corners_out(d)
            elif j in (0, chunks - 1):
                @pl.when((mirrored == (1 if d > 0 else 0)) == (j == 0))
                def _(d=d):
                    corners_out(d)

    events = ((0, send, 1), (1, send, 2), (2, send, 3), (5, pass_on, 0), (6, pass_on, 1), (6, pass_on, 2), (6, pass_on, 3))
    step = 2 if X % 2 == 0 else 1

    def poll(point):
        for when_at, act, j in events:
            if j < chunks:
                @pl.when(point == when_at)
                def _(act=act, j=j):
                    act(j)

    if X == 1:
        ends = ((0, (0,)),)
    else:
        ends = ((0, (0, 1)), (X - 1, (-1, 0)))
    for h in range(WGROUPS):
        planes(ends[0][0], 1, ends[0][1], h, True)
    if X > 2:
        @pl.loop(0, (X - 2) // step)
        def _(i):
            for h in range(WGROUPS):
                poll(WGROUPS * i + h)
                planes(1 + step * i, step, (-1, 0, 1), h, True)
    for x, offsets in ends[1:]:
        for h in range(WGROUPS):
            planes(x, 1, offsets, h, True)
    reached = WGROUPS * ((X - 2) // step) if X > 2 else 0
    for when_at, act, j in events:
        if j < chunks and when_at >= reached:
            act(j)
    arrived(0)

    for d in (-1, 1):
        @pl.when(has_x(d))
        def _(d=d):
            x_copy(-d).wait_recv()
            px = 0 if d < 0 else X + 1
            for py in range(1, Y + 1):
                shifted(px, py)
            for h in range(WGROUPS):
                planes(0 if d < 0 else X - 1, 1, (d,), h, False)

    def add_row(px0, n, py, x0, a):
        b = jnp.where(py == 0, 0, 2)
        row = pl.ds(pl.multiple_of(jnp.where(py == 0, 0, Y - 1) * Z, Z), Z)
        lhs = xs[pl.ds(px0, n), py].reshape(n * Z, 3 * C)
        w = wd[pl.ds(((a + 1) * 3 + b) * 3, 3)].reshape(3 * C, C)
        acc[pl.ds(x0 + 1, n), row] += fma(lhs, w).reshape(n, Z, C)

    def take(j, p, py):
        for q in range(CH):
            shifted(p + 1 + q, py)
        for a in (-1, 0, 1):
            add_row(p + 1, CH, py, p - a, a)

    def corners_in(d, near):
        here = has_x(d) & ((mirrored == (1 if d > 0 else 0)) == near)
        for side, (py, ok) in enumerate(sides):
            @pl.when(here if ok is True else here & ok)
            def _(side=side, py=py):
                corner_copy(-d, side, py).wait_recv()
                px = 0 if d < 0 else X + 1
                shifted(px, py)
                add_row(px, 1, py, 0 if d < 0 else X - 1, d)

    def add_moments(h):
        for g in range(WGROUPS):
            at = pl.ds(g * WG, WG)
            v = h[:, g * WG:(g + 1) * WG]
            gram[at] += lax.dot_general(v, v, (((0,), (0,)), ((), ())), preferred_element_type=F32)
            sums[:, at] += jnp.sum(v.astype(F32).reshape(-1, 8, WG), axis=0)

    edge_rows = [pl.ds(0, Z), pl.ds((Y - 1) * Z, Z)][:Y]

    def inner_moments(x, n):
        at = pl.ds(Z, (Y - 2) * Z)
        h = acc[pl.ds(x + 1, n), at].astype(BF16)
        hid[pl.ds(x, n), at] = h
        add_moments(h.reshape(-1, C))

    def edge_moments(q, n):
        x = jnp.where(mirrored == 1, X - q - n, q)
        parts = []
        for at in edge_rows:
            h = acc[pl.ds(x + 1, n), at].astype(BF16)
            hid[pl.ds(x, n), at] = h
            parts.append(h.reshape(-1, C))
        add_moments(jnp.concatenate(parts, axis=0))

    gram[...] = jnp.zeros_like(gram)
    sums[...] = jnp.zeros_like(sums)
    if Y > 2:
        group = 4 if X % 4 == 0 else 1

        @pl.loop(0, X // group)
        def _(i):
            inner_moments(group * i, group)
    early = max(0, (chunks - 1) * CH - 1)
    sooner = max(0, (chunks - 2) * CH - 1)
    for j in range(chunks):
        p = plane_of(j)
        if j == chunks - 1:
            if chunks > 1 and not sooner:
                for d in (-1, 1):
                    corners_in(d, True)
            if early:
                edge_moments(sooner, early - sooner)
        if j and j == chunks - 2 and sooner:
            for d in (-1, 1):
                corners_in(d, True)
            edge_moments(0, sooner)
        if j:
            arrived(j)
        for py, ok in sides:
            @when(ok)
            def _(j=j, p=p, py=py):
                take(j, p, py)
    for d in (-1, 1):
        if chunks == 1:
            corners_in(d, True)
        corners_in(d, False)
    edge_moments(early, X - early)

    mine = me_d == 0
    H = WG // 2
    half = lax.broadcasted_iota(jnp.int32, (H // 2, WG), 1) < H

    def packed(g):
        tail = gram[pl.ds(g * WG + H, H)]
        across = jnp.where(half, pltpu.roll(tail[:H // 2], H, 1), tail[H // 2:])
        return gram[pl.ds(g * WG, H)], across, sums[:, pl.ds(g * WG, WG)]

    places = (pl.ds(0, H), pl.ds(H, H // 2), pl.ds(H + H // 2, 8))
    low, high = packed(0), packed(1)
    for place, a, b in zip(places, low, high):
        give[place] = jnp.where(mine, b, a)
    swap = pltpu.make_async_remote_copy(
        src_ref=give, dst_ref=got_pair, send_sem=pair_send.at[0], recv_sem=pair_recv.at[0],
        device_id=pair, device_id_type=MESH)
    swap.start()
    for place, a, b in zip(places, low, high):
        red[0, place] = jnp.where(mine, a, b)
    swap.wait()
    red[0] += got_pair[...]

    count = len(stages)

    def legs(step, stream):
        part = pl.ds(*parts[stream])
        return [
            pltpu.make_async_remote_copy(
                src_ref=red.at[step, part], dst_ref=got.at[step, i, part],
                send_sem=tree_send.at[step, stream, i], recv_sem=tree_recv.at[step, stream, i],
                device_id=flips(bits), device_id_type=MESH)
            for i, bits in enumerate(subsets(stages[(step + stream) % count]))]

    def send_sums(step, stream):
        for leg in reversed(legs(step, stream)):
            leg.start()

    for stream in range(len(parts)):
        send_sums(0, stream)
    for step in range(count):
        for stream in range(len(parts)):
            for leg in legs(step, stream):
                leg.wait_recv()
            part = pl.ds(*parts[stream])
            total = red[step, part] + got[step, 0, part]
            if len(stages[(step + stream) % count]) > 1:
                total += got[step, 1, part] + got[step, 2, part]
            red[step + 1, part] = total
            if step + 1 < count:
                send_sums(step + 1, stream)

    average = jnp.sum(red[count, places[2]], axis=0, keepdims=True) / whole_count
    across = jnp.broadcast_to(average, (WG, WG))
    down = across.T
    top, tail = red[count, places[0]], red[count, places[1]]
    right = jnp.concatenate([top, pltpu.roll(tail, H, 1), tail], axis=0)
    left = lax.broadcasted_iota(jnp.int32, (WG, WG), 1) < H
    lower = lax.broadcasted_iota(jnp.int32, (WG, WG), 0) >= H
    moment = jnp.where(left & lower, right.T, right)
    covariance = moment / whole_count - down * across
    identity = jnp.where(
        lax.broadcasted_iota(jnp.int32, (WG, WG), 0) == lax.broadcasted_iota(jnp.int32, (WG, WG), 1),
        1.0, 0.0).astype(F32)
    moved = covariance + epsilon * identity
    square = jnp.sum(jnp.sum(moved * moved, axis=1, keepdims=True), axis=0, keepdims=True)
    frobenius = jnp.sqrt(square)
    y = moved / frobenius
    z = None
    for number in range(STEPS):
        p = 1.5 * identity - 0.5 * (y if z is None else fdot(z, y))
        if number < STEPS - 1:
            y = fdot(y, p)
        z = p if z is None else fdot(p, z)
    whitener = z / jnp.sqrt(frobenius)
    turned = whitener.astype(BF16).astype(F32)
    fin[pl.ds(0, WG)] = turned
    fin[pl.ds(WG, 8)] = jnp.broadcast_to(jnp.sum(turned * down, axis=0, keepdims=True), (8, WG))
    swap = pltpu.make_async_remote_copy(
        src_ref=fin, dst_ref=got_fin, send_sem=pair_send.at[1], recv_sem=pair_recv.at[1],
        device_id=pair, device_id_type=MESH)
    swap.start()
    own = fin[...]
    swap.wait()
    other = got_fin[...]
    first = jnp.where(mine, own, other)
    second = jnp.where(mine, other, own)
    white_ref[...] = jnp.zeros_like(white_ref)
    white_ref[pl.ds(0, WG), pl.ds(0, WG)] = first[:WG].astype(BF16)
    white_ref[pl.ds(WG, WG), pl.ds(WG, WG)] = second[:WG].astype(BF16)
    shift_ref[:, pl.ds(0, WG)] = first[WG:]
    shift_ref[:, pl.ds(WG, WG)] = second[WG:]

    for step in range(count):
        for stream in range(len(parts)):
            for leg in legs(step, stream):
                leg.wait_send()
    for j in range(chunks):
        to_direct_copy(j).wait_send()

        @pl.when(has_diag)
        def _(j=j):
            to_diag_copy(j).wait_send()

        @pl.when(j < to_pass)
        def _(j=j):
            onward_copy(j).wait_send()
    for d in (-1, 1):
        @pl.when(has_x(d))
        def _(d=d):
            x_copy(d).wait_send()
        for side, (py, ok) in enumerate(sides):
            @pl.when(has_x(d) if ok is True else has_x(d) & ok)
            def _(d=d, side=side, py=py):
                corner_copy(d, side, py).wait_send()


def apply_kernel(h_ref, w_ref, s_ref, o_ref, block, sems):
    X = h_ref.shape[0]
    copies = [pltpu.make_async_copy(block.at[x], o_ref.at[x], sems.at[x]) for x in range(X)]
    for x in range(X):
        result = fma(h_ref[x], w_ref[...]) - s_ref[0:1, :]
        block[x] = result.astype(BF16).reshape(block.shape[1:])
        copies[x].start()
    for copy in copies:
        copy.wait()


def on_device(sizes, volume, kernel):
    nd, nx, ny = sizes
    X, Y, Z, C = volume.shape[1:]
    GC = kernel.shape[3]
    WG = C // WGROUPS
    stages = []
    for axis, n in (("sx", nx), ("syz", ny)):
        bit = 1
        while bit < n:
            stages.append((axis, bit))
            bit *= 2
    stages = [tuple(stages[i:i + 2]) for i in range(0, len(stages), 2)]
    streams = len(stages)
    blocks = (3 * WG // 4 + 8) // 8
    edges = [8 * (blocks * i // streams) for i in range(streams + 1)]
    parts = [(edges[i], edges[i + 1] - edges[i]) for i in range(streams)]
    whole_count = float(X * Y * Z * nd * nx * ny)
    R = 3 * WG // 4 + 8
    count = len(stages)
    dma = pltpu.SemaphoreType.DMA
    chunks = max(n for n in (1, 2, 4) if X % n == 0)
    hidden, white, shift = pl.pallas_call(
        functools.partial(main_kernel, (nx, ny), tuple(stages), tuple(parts), whole_count, chunks),
        out_shape=(
            pltpu.VMEM((X, Y * Z, C), BF16),
            pltpu.VMEM((C, C), BF16),
            pltpu.VMEM((8, C), F32),
        ),
        in_specs=[pl.BlockSpec(memory_space=pl.ANY), pl.BlockSpec(memory_space=pltpu.VMEM)],
        out_specs=(
            pl.BlockSpec(memory_space=pltpu.VMEM),
            pl.BlockSpec(memory_space=pltpu.VMEM),
            pl.BlockSpec(memory_space=pltpu.VMEM),
        ),
        scratch_shapes=[
            pltpu.VMEM((X + 2, Y + 2, Z, 3 * C), BF16),
            pltpu.VMEM((27, C, C), BF16),
            pltpu.VMEM((WGROUPS, 3, 4, 3 * WG, 2 * WG), BF16),
            pltpu.VMEM((X + 2, Y * Z, C), F32),
            pltpu.VMEM((chunks, X // chunks, Z, C), BF16),
            pltpu.VMEM((C, WG), F32),
            pltpu.VMEM((8, C), F32),
            pltpu.VMEM((count + 1, R, WG), F32),
            pltpu.VMEM((count, 3, R, WG), F32),
            pltpu.VMEM((R, WG), F32),
            pltpu.VMEM((R, WG), F32),
            pltpu.VMEM((WG + 8, WG), F32),
            pltpu.VMEM((WG + 8, WG), F32),
            dma, dma((chunks,)), dma((chunks,)), dma((chunks,)), dma((chunks,)), dma((chunks,)), dma((chunks,)),
            dma((2,)), dma((2,)), dma((2, 2)), dma((2, 2)),
            dma((2,)), dma((2,)), dma((count, streams, 3)), dma((count, streams, 3)),
        ],
        compiler_params=pltpu.CompilerParams(
            collective_id=0, has_side_effects=True, vmem_limit_bytes=56 * 2**20),
        name="conv_moments",
    )(volume, kernel.reshape(27, GC, C))
    result = pl.pallas_call(
        apply_kernel,
        out_shape=jax.ShapeDtypeStruct((X, Y, Z, C), BF16),
        in_specs=[pl.BlockSpec(memory_space=pltpu.VMEM)] * 3,
        out_specs=pl.BlockSpec(memory_space=pl.ANY),
        scratch_shapes=[pltpu.VMEM((X, Y, Z, C), BF16), dma((X,))],
        name="apply",
    )(*(pltpu.with_memory_space_constraint(v, pltpu.VMEM) for v in (hidden, white, shift)))
    return result.reshape(volume.shape)


def solution(mesh):
    sizes = (mesh.shape["dp"], mesh.shape["sx"], mesh.shape["syz"])
    placed = (P("dp", "sx", "syz", None, None), P())
    return jax.shard_map(
        functools.partial(on_device, sizes),
        mesh=mesh,
        in_specs=placed,
        out_specs=P("dp", "sx", "syz", None, None),
        check_vma=False,
    )
```

```python
import functools

import jax
import jax.numpy as jnp
from jax import lax
from jax.experimental import pallas as pl
from jax.experimental.pallas import tpu as pltpu
from jax.sharding import PartitionSpec as P

WGROUPS = 2
STEPS = 5
epsilon = 1e-05
highest = lax.Precision.HIGHEST
MESH = pl.DeviceIdType.MESH
F32 = jnp.float32
BF16 = jnp.bfloat16


def fma(a, b):
    return jnp.dot(a, b, preferred_element_type=F32)


def fdot(a, b):
    def halves(m):
        top = m.astype(BF16)
        return top, (m - top.astype(F32)).astype(BF16)

    n = b.shape[1]
    left = jnp.concatenate(halves(a), axis=1)
    right = jnp.concatenate(halves(b), axis=1)
    both = fma(left, jnp.concatenate([right, right], axis=0))
    return both[:, :n] + both[:, n:]


def subsets(stage):
    return [stage] if len(stage) == 1 else [stage[:1], stage[1:], stage]


def main_kernel(
    sizes, stages, parts, whole_count, chunks,
    v_ref, k_ref, hid, white_ref, shift_ref,
    xs, wd, wt, acc, passing, gram, sums, red, got, give, got_pair, fin, got_fin,
    load_sem, send_dir, recv_dir, send_diag, recv_diag, send_pass, recv_pass,
    send_x, recv_x, send_c, recv_c,
    pair_send, pair_recv, tree_send, tree_recv,
):
    nx, ny = sizes
    X, Y, Z, C = v_ref.shape[1:]
    GC = k_ref.shape[1]
    WG = C // WGROUPS
    CH = X // chunks
    me_d = lax.axis_index("dp")
    me_x = lax.axis_index("sx")
    me_y = lax.axis_index("syz")

    def flips(bits):
        where = {}
        for axis, bit in bits:
            me = lax.axis_index(axis)
            where[axis] = where.get(axis, me) + bit - 2 * bit * ((me // bit) % 2)
        return where

    load = pltpu.make_async_copy(
        v_ref.at[0], xs.at[pl.ds(1, X), pl.ds(1, Y), :, pl.ds(C, C)], load_sem)
    load.start()

    odd = me_y % 2
    sign = 2 * odd - 1
    direct, diagonal = me_y - sign, me_y + sign
    behind, ahead = me_y - 2 * sign, me_y + 2 * sign

    def inside(v):
        return (v >= 0) & (v < ny)

    def rerouted(i):
        m = i // 2
        pairs = ny // 2
        return (chunks * jnp.where(i % 2 == 1, pairs - 1 - m, m)) // pairs

    def has_x(d):
        return (me_x + d >= 0) & (me_x + d < nx)

    has_diag = inside(diagonal)
    my_rerouted = jnp.where(has_diag, rerouted(me_y), 0)
    to_pass = jnp.where(inside(behind), rerouted(direct), 0)
    mirrored = (me_x + 1) % 2

    barrier = pltpu.get_barrier_semaphore()

    def greet(where):
        pl.semaphore_signal(barrier, inc=1, device_id=where, device_id_type=MESH)

    pair = flips((("dp", 1),))
    far = [flips(bits) for stage in reversed(stages) for bits in reversed(subsets(stage))] + [pair]
    for who in far:
        greet(who)
    greeted = 0
    other = [(has_x(d) & (me_x % 2 == (0 if d < 0 else 1)), {"sx": me_x + d}) for d in (-1, 1)] if nx > 2 else []
    for ok, where in [
        (has_diag, {"syz": diagonal}),
        (inside(behind), {"syz": behind}),
        (inside(ahead), {"syz": ahead}),
    ] + other:
        @pl.when(ok)
        def _(where=where):
            greet(where)
        greeted += jnp.where(ok, 1, 0)

    lanes = lax.broadcasted_iota(jnp.int32, (GC, C), 1) // GC
    wt[:, :, 0, :, pl.ds(WG, WG)] = jnp.zeros((WGROUPS, 3, 3 * WG, WG), BF16)
    wt[:, :, 3, :, pl.ds(0, WG)] = jnp.zeros((WGROUPS, 3, 3 * WG, WG), BF16)

    @pl.loop(0, k_ref.shape[0])
    def _(t):
        w = k_ref[t].astype(F32)
        for g in range(C // GC):
            masked = jnp.where(lanes == g, w, 0.0).astype(BF16)
            wd[t, pl.ds(g * GC, GC), :] = masked
            h = g * GC // WG
            at = pl.ds(pl.multiple_of((t % 3) * WG + g * GC - h * WG, GC), GC)
            part = masked[:, h * WG:(h + 1) * WG]
            wt[h, t // 9, (t // 3) % 3, at, pl.ds(0, WG)] = part
            wt[h, t // 9, (t // 3) % 3 + 1, at, pl.ds(WG, WG)] = part

    pl.semaphore_wait(barrier, greeted + len(far))

    def plane_of(j):
        return jnp.where(mirrored == 1, X - (j + 1) * CH, j * CH)

    row_direct, row_diag = (Y - 1) * (1 - odd), (Y - 1) * odd
    to_direct, to_diag = (Y + 1) * odd, (Y + 1) * (1 - odd)
    in_direct, in_diag = (Y + 1) * (1 - odd), (Y + 1) * odd

    def middle(px, py):
        return xs.at[px, py, :, pl.ds(C, C)]

    def to_direct_copy(j):
        p = plane_of(j)
        return pltpu.make_async_remote_copy(
            src_ref=v_ref.at[0, pl.ds(p, CH), row_direct],
            dst_ref=middle(pl.ds(p + 1, CH), to_direct),
            send_sem=send_dir.at[j], recv_sem=recv_dir.at[j],
            device_id={"syz": direct}, device_id_type=MESH)

    def to_diag_copy(j):
        p = plane_of(j)
        return pltpu.make_async_remote_copy(
            src_ref=v_ref.at[0, pl.ds(p, CH), row_diag],
            dst_ref=middle(pl.ds(p + 1, CH), to_diag),
            send_sem=send_diag.at[j], recv_sem=recv_diag.at[j],
            device_id={"syz": diagonal}, device_id_type=MESH)

    def detour_copy(j):
        return pltpu.make_async_remote_copy(
            src_ref=v_ref.at[0, pl.ds(plane_of(j), CH), row_diag],
            dst_ref=passing.at[j],
            send_sem=send_diag.at[j], recv_sem=recv_pass.at[j],
            device_id={"syz": direct}, device_id_type=MESH)

    def onward_copy(j):
        return pltpu.make_async_remote_copy(
            src_ref=passing.at[j],
            dst_ref=middle(pl.ds(plane_of(j) + 1, CH), to_direct),
            send_sem=send_pass.at[j], recv_sem=recv_diag.at[j],
            device_id={"syz": behind}, device_id_type=MESH)

    def x_copy(d):
        i = (d + 1) // 2
        return pltpu.make_async_remote_copy(
            src_ref=v_ref.at[0, 0 if d < 0 else X - 1],
            dst_ref=middle(X + 1 if d < 0 else 0, pl.ds(1, Y)),
            send_sem=send_x.at[i], recv_sem=recv_x.at[1 - i],
            device_id={"sx": me_x + d}, device_id_type=MESH)

    def corner_copy(d, side, py):
        i = (d + 1) // 2
        return pltpu.make_async_remote_copy(
            src_ref=middle(1 if d < 0 else X, py),
            dst_ref=middle(X + 1 if d < 0 else 0, py),
            send_sem=send_c.at[i, side], recv_sem=recv_c.at[1 - i, side],
            device_id={"sx": me_x + d}, device_id_type=MESH)

    for j in range(chunks):
        @pl.when(j < my_rerouted)
        def _(j=j):
            detour_copy(j).start()
    for d in (-1, 1):
        @pl.when(has_x(d))
        def _(d=d):
            x_copy(d).start()
    def send(j):
        to_direct_copy(j).start()

        @pl.when(has_diag & (j >= my_rerouted))
        def _():
            to_diag_copy(j).start()

    send(0)

    def pass_on(j):
        @pl.when(j < to_pass)
        def _():
            detour_copy(j).wait_recv()
            onward_copy(j).start()

    rows = lax.broadcasted_iota(jnp.int32, (Z, C), 0)

    def shifted(px, py):
        v = xs[px, py, :, pl.ds(C, C)].astype(F32)
        xs[px, py, :, pl.ds(0, C)] = jnp.where(rows == 0, 0.0, pltpu.roll(v, 1, 0)).astype(BF16)
        xs[px, py, :, pl.ds(2 * C, C)] = jnp.where(
            rows == Z - 1, 0.0, pltpu.roll(v, Z - 1, 0)).astype(BF16)

    load.wait()

    @pl.loop(1, X + 1)
    def _(px):
        for py in range(1, Y + 1):
            shifted(px, py)

    def planes(x, n, offsets, h, fresh):
        for t in range(Y // 2):
            rows = [p for p in range(2 * t - 1, 2 * t + 3) if 0 <= p < Y]
            low = rows[0] - (2 * t - 1)
            def operand(a):
                return [xs[pl.ds(x + 1 + a, n), p + 1, :, pl.ds(c * C + h * WG, WG)].reshape(n * Z, WG)
                        for p in rows for c in range(3)]

            def factor(a):
                return wt[h, a + 1, pl.ds(low, len(rows))].reshape(len(rows) * 3 * WG, 2 * WG)

            both = fma(
                jnp.concatenate([v for a in offsets for v in operand(a)], axis=1),
                jnp.concatenate([factor(a) for a in offsets], axis=0))
            for u in range(2):
                at = (pl.ds(x + 1, n), pl.ds((2 * t + u) * Z, Z), pl.ds(h * WG, WG))
                value = both[:, u * WG:(u + 1) * WG].reshape(n, Z, WG)
                if fresh:
                    acc[at] = value
                else:
                    acc[at] += value

    sides = ((in_direct, True), (in_diag, has_diag))

    def when(ok):
        return (lambda f: f()) if ok is True else pl.when(ok)

    def corners_out(d):
        for side, (py, ok) in enumerate(sides):
            @pl.when(has_x(d) if ok is True else has_x(d) & ok)
            def _(side=side, py=py):
                corner_copy(d, side, py).start()

    def arrived(j):
        to_direct_copy(j).wait_recv()

        @pl.when(has_diag)
        def _():
            to_diag_copy(j).wait_recv()
        for d in (-1, 1):
            if chunks == 1:
                corners_out(d)
            elif j in (0, chunks - 1):
                @pl.when((mirrored == (1 if d > 0 else 0)) == (j == 0))
                def _(d=d):
                    corners_out(d)

    events = ((0, send, 1), (0, send, 2), (0, send, 3), (4, pass_on, 0), (6, pass_on, 1), (6, pass_on, 2), (6, pass_on, 3))
    step = 2 if X % 2 == 0 else 1

    def poll(point):
        for when_at, act, j in events:
            if j < chunks:
                @pl.when(point == when_at)
                def _(act=act, j=j):
                    act(j)

    if X == 1:
        ends = ((0, (0,)),)
    else:
        ends = ((0, (0, 1)), (X - 1, (-1, 0)))
    for h in range(WGROUPS):
        planes(ends[0][0], 1, ends[0][1], h, True)
    if X > 2:
        @pl.loop(0, (X - 2) // step)
        def _(i):
            for h in range(WGROUPS):
                poll(WGROUPS * i + h)
                planes(1 + step * i, step, (-1, 0, 1), h, True)
    for x, offsets in ends[1:]:
        for h in range(WGROUPS):
            planes(x, 1, offsets, h, True)
    reached = WGROUPS * ((X - 2) // step) if X > 2 else 0
    for when_at, act, j in events:
        if j < chunks and when_at >= reached:
            act(j)
    arrived(0)

    for d in (-1, 1):
        @pl.when(has_x(d))
        def _(d=d):
            x_copy(-d).wait_recv()
            px = 0 if d < 0 else X + 1
            for py in range(1, Y + 1):
                shifted(px, py)
            for h in range(WGROUPS):
                planes(0 if d < 0 else X - 1, 1, (d,), h, False)

    def add_row(px0, n, py, x0, a):
        b = jnp.where(py == 0, 0, 2)
        row = pl.ds(pl.multiple_of(jnp.where(py == 0, 0, Y - 1) * Z, Z), Z)
        lhs = xs[pl.ds(px0, n), py].reshape(n * Z, 3 * C)
        w = wd[pl.ds(((a + 1) * 3 + b) * 3, 3)].reshape(3 * C, C)
        acc[pl.ds(x0 + 1, n), row] += fma(lhs, w).reshape(n, Z, C)

    def take(j, p, py):
        for q in range(CH):
            shifted(p + 1 + q, py)
        for a in (-1, 0, 1):
            add_row(p + 1, CH, py, p - a, a)

    def corners_in(d, near):
        here = has_x(d) & ((mirrored == (1 if d > 0 else 0)) == near)
        for side, (py, ok) in enumerate(sides):
            @pl.when(here if ok is True else here & ok)
            def _(side=side, py=py):
                corner_copy(-d, side, py).wait_recv()
                px = 0 if d < 0 else X + 1
                shifted(px, py)
                add_row(px, 1, py, 0 if d < 0 else X - 1, d)

    def add_moments(h):
        for g in range(WGROUPS):
            at = pl.ds(g * WG, WG)
            v = h[:, g * WG:(g + 1) * WG]
            gram[at] += lax.dot_general(v, v, (((0,), (0,)), ((), ())), preferred_element_type=F32)
            sums[:, at] += jnp.sum(v.astype(F32).reshape(-1, 8, WG), axis=0)

    edge_rows = [pl.ds(0, Z), pl.ds((Y - 1) * Z, Z)][:Y]

    def inner_moments(x, n):
        at = pl.ds(Z, (Y - 2) * Z)
        h = acc[pl.ds(x + 1, n), at].astype(BF16)
        hid[pl.ds(x, n), at] = h
        add_moments(h.reshape(-1, C))

    def edge_moments(q, n):
        x = jnp.where(mirrored == 1, X - q - n, q)
        parts = []
        for at in edge_rows:
            h = acc[pl.ds(x + 1, n), at].astype(BF16)
            hid[pl.ds(x, n), at] = h
            parts.append(h.reshape(-1, C))
        add_moments(jnp.concatenate(parts, axis=0))

    gram[...] = jnp.zeros_like(gram)
    sums[...] = jnp.zeros_like(sums)
    if Y > 2:
        group = 4 if X % 4 == 0 else 1

        @pl.loop(0, X // group)
        def _(i):
            inner_moments(group * i, group)
    early = max(0, (chunks - 1) * CH - 1)
    sooner = max(0, (chunks - 2) * CH - 1)
    for j in range(chunks):
        p = plane_of(j)
        if j == chunks - 1:
            if chunks > 1 and not sooner:
                for d in (-1, 1):
                    corners_in(d, True)
            if early:
                edge_moments(sooner, early - sooner)
        if j and j == chunks - 2 and sooner:
            for d in (-1, 1):
                corners_in(d, True)
            edge_moments(0, sooner)
        if j:
            arrived(j)
        for py, ok in sides:
            @when(ok)
            def _(j=j, p=p, py=py):
                take(j, p, py)
    for d in (-1, 1):
        if chunks == 1:
            corners_in(d, True)
        corners_in(d, False)
    edge_moments(early, X - early)

    mine = me_d == 0
    H, Q = WG // 2, WG // 4
    lane_of = lax.broadcasted_iota(jnp.int32, (Q, WG), 1)

    def packed(g):
        row = [gram[pl.ds(g * WG + i * Q, Q)] for i in range(4)]
        mixed = jnp.where(lane_of < Q, pltpu.roll(row[3], Q, 1), row[1])
        folded = jnp.where(lane_of[:Q // 2] < H, pltpu.roll(row[2][:Q // 2], H, 1), row[2][Q // 2:])
        return row[0], mixed, folded, sums[:, pl.ds(g * WG, WG)]

    places = (pl.ds(0, Q), pl.ds(Q, Q), pl.ds(2 * Q, Q // 2), pl.ds(2 * Q + Q // 2, 8))
    low, high = packed(0), packed(1)
    for place, a, b in zip(places, low, high):
        give[place] = jnp.where(mine, b, a)
    swap = pltpu.make_async_remote_copy(
        src_ref=give, dst_ref=got_pair, send_sem=pair_send.at[0], recv_sem=pair_recv.at[0],
        device_id=pair, device_id_type=MESH)
    swap.start()
    for place, a, b in zip(places, low, high):
        red[0, place] = jnp.where(mine, a, b)
    swap.wait()
    red[0] += got_pair[...]

    count = len(stages)

    def legs(step, stream):
        part = pl.ds(*parts[stream])
        return [
            pltpu.make_async_remote_copy(
                src_ref=red.at[step, part], dst_ref=got.at[step, i, part],
                send_sem=tree_send.at[step, stream, i], recv_sem=tree_recv.at[step, stream, i],
                device_id=flips(bits), device_id_type=MESH)
            for i, bits in enumerate(subsets(stages[(step + stream) % count]))]

    def send_sums(step, stream):
        for leg in reversed(legs(step, stream)):
            leg.start()

    for stream in reversed(range(len(parts))):
        send_sums(0, stream)
    for j in range(chunks):
        to_direct_copy(j).wait_send()

        @pl.when(has_diag)
        def _(j=j):
            to_diag_copy(j).wait_send()

        @pl.when(j < to_pass)
        def _(j=j):
            onward_copy(j).wait_send()
    for d in (-1, 1):
        @pl.when(has_x(d))
        def _(d=d):
            x_copy(d).wait_send()
        for side, (py, ok) in enumerate(sides):
            @pl.when(has_x(d) if ok is True else has_x(d) & ok)
            def _(d=d, side=side, py=py):
                corner_copy(d, side, py).wait_send()
    white_ref[...] = jnp.zeros_like(white_ref)
    for step in range(count):
        for stream in range(len(parts)):
            for leg in legs(step, stream):
                leg.wait_recv()
            part = pl.ds(*parts[stream])
            total = red[step, part] + got[step, 0, part]
            if len(stages[(step + stream) % count]) > 1:
                total += got[step, 1, part] + got[step, 2, part]
            red[step + 1, part] = total
            if step + 1 < count:
                send_sums(step + 1, stream)

    average = jnp.sum(red[count, places[3]], axis=0, keepdims=True) / whole_count
    across = jnp.broadcast_to(average, (WG, WG))
    down = across.T
    top, mixed, folded = (red[count, place] for place in places[:3])
    right = jnp.concatenate([top, mixed, pltpu.roll(folded, H, 1), folded, pltpu.roll(mixed, WG - Q, 1)], axis=0)
    column = lax.broadcasted_iota(jnp.int32, (WG, WG), 1) // Q
    moment = jnp.where(column < lax.broadcasted_iota(jnp.int32, (WG, WG), 0) // Q, right.T, right)
    covariance = moment / whole_count - down * across
    identity = jnp.where(
        lax.broadcasted_iota(jnp.int32, (WG, WG), 0) == lax.broadcasted_iota(jnp.int32, (WG, WG), 1),
        1.0, 0.0).astype(F32)
    moved = covariance + epsilon * identity
    square = jnp.sum(jnp.sum(moved * moved, axis=1, keepdims=True), axis=0, keepdims=True)
    frobenius = jnp.sqrt(square)
    y = moved / frobenius
    z = None
    for number in range(STEPS):
        p = 1.5 * identity - 0.5 * (y if z is None else fdot(z, y))
        if number < STEPS - 1:
            y = fdot(y, p)
        z = p if z is None else fdot(p, z)
    whitener = z / jnp.sqrt(frobenius)
    turned = whitener.astype(BF16).astype(F32)
    fin[pl.ds(0, WG)] = turned
    fin[pl.ds(WG, 8)] = jnp.broadcast_to(jnp.sum(turned * down, axis=0, keepdims=True), (8, WG))
    swap = pltpu.make_async_remote_copy(
        src_ref=fin, dst_ref=got_fin, send_sem=pair_send.at[1], recv_sem=pair_recv.at[1],
        device_id=pair, device_id_type=MESH)
    swap.start()
    own = fin[...]
    for step in range(count):
        for stream in range(len(parts)):
            for leg in legs(step, stream):
                leg.wait_send()
    swap.wait()
    other = got_fin[...]
    first = jnp.where(mine, own, other)
    second = jnp.where(mine, other, own)
    white_ref[pl.ds(0, WG), pl.ds(0, WG)] = first[:WG].astype(BF16)
    white_ref[pl.ds(WG, WG), pl.ds(WG, WG)] = second[:WG].astype(BF16)
    shift_ref[:, pl.ds(0, WG)] = first[WG:]
    shift_ref[:, pl.ds(WG, WG)] = second[WG:]


def apply_kernel(h_ref, w_ref, s_ref, o_ref, block, sems):
    X = h_ref.shape[0]
    copies = [pltpu.make_async_copy(block.at[x], o_ref.at[x], sems.at[x]) for x in range(X)]
    for x in range(X):
        result = fma(h_ref[x], w_ref[...]) - s_ref[0:1, :]
        block[x] = result.astype(BF16).reshape(block.shape[1:])
        copies[x].start()
    for copy in copies:
        copy.wait()


def on_device(sizes, volume, kernel):
    nd, nx, ny = sizes
    X, Y, Z, C = volume.shape[1:]
    GC = kernel.shape[3]
    WG = C // WGROUPS
    stages = []
    for axis, n in (("sx", nx), ("syz", ny)):
        bit = 1
        while bit < n:
            stages.append((axis, bit))
            bit *= 2
    stages = [tuple(stages[i:i + 2]) for i in range(0, len(stages), 2)]
    streams = len(stages)
    R = 5 * WG // 8 + 8
    blocks = R // 8
    edges = [8 * (blocks * i // streams) for i in range(streams + 1)]
    parts = [(edges[i], edges[i + 1] - edges[i]) for i in range(streams)]
    whole_count = float(X * Y * Z * nd * nx * ny)
    count = len(stages)
    dma = pltpu.SemaphoreType.DMA
    chunks = max(n for n in (1, 2, 4) if X % n == 0)
    hidden, white, shift = pl.pallas_call(
        functools.partial(main_kernel, (nx, ny), tuple(stages), tuple(parts), whole_count, chunks),
        out_shape=(
            pltpu.VMEM((X, Y * Z, C), BF16),
            pltpu.VMEM((C, C), BF16),
            pltpu.VMEM((8, C), F32),
        ),
        in_specs=[pl.BlockSpec(memory_space=pl.ANY), pl.BlockSpec(memory_space=pltpu.VMEM)],
        out_specs=(
            pl.BlockSpec(memory_space=pltpu.VMEM),
            pl.BlockSpec(memory_space=pltpu.VMEM),
            pl.BlockSpec(memory_space=pltpu.VMEM),
        ),
        scratch_shapes=[
            pltpu.VMEM((X + 2, Y + 2, Z, 3 * C), BF16),
            pltpu.VMEM((27, C, C), BF16),
            pltpu.VMEM((WGROUPS, 3, 4, 3 * WG, 2 * WG), BF16),
            pltpu.VMEM((X + 2, Y * Z, C), F32),
            pltpu.VMEM((chunks, X // chunks, Z, C), BF16),
            pltpu.VMEM((C, WG), F32),
            pltpu.VMEM((8, C), F32),
            pltpu.VMEM((count + 1, R, WG), F32),
            pltpu.VMEM((count, 3, R, WG), F32),
            pltpu.VMEM((R, WG), F32),
            pltpu.VMEM((R, WG), F32),
            pltpu.VMEM((WG + 8, WG), F32),
            pltpu.VMEM((WG + 8, WG), F32),
            dma, dma((chunks,)), dma((chunks,)), dma((chunks,)), dma((chunks,)), dma((chunks,)), dma((chunks,)),
            dma((2,)), dma((2,)), dma((2, 2)), dma((2, 2)),
            dma((2,)), dma((2,)), dma((count, streams, 3)), dma((count, streams, 3)),
        ],
        compiler_params=pltpu.CompilerParams(
            collective_id=0, has_side_effects=True, vmem_limit_bytes=56 * 2**20),
        name="conv_moments",
    )(volume, kernel.reshape(27, GC, C))
    result = pl.pallas_call(
        apply_kernel,
        out_shape=jax.ShapeDtypeStruct((X, Y, Z, C), BF16),
        in_specs=[pl.BlockSpec(memory_space=pltpu.VMEM)] * 3,
        out_specs=pl.BlockSpec(memory_space=pl.ANY),
        scratch_shapes=[pltpu.VMEM((X, Y, Z, C), BF16), dma((X,))],
        name="apply",
    )(*(pltpu.with_memory_space_constraint(v, pltpu.VMEM) for v in (hidden, white, shift)))
    return result.reshape(volume.shape)


def solution(mesh):
    sizes = (mesh.shape["dp"], mesh.shape["sx"], mesh.shape["syz"])
    placed = (P("dp", "sx", "syz", None, None), P())
    return jax.shard_map(
        functools.partial(on_device, sizes),
        mesh=mesh,
        in_specs=placed,
        out_specs=P("dp", "sx", "syz", None, None),
        check_vma=False,
    )
```

```python
import functools

import jax
import jax.numpy as jnp
from jax import lax
from jax.experimental import pallas as pl
from jax.experimental.pallas import tpu as pltpu
from jax.sharding import PartitionSpec as P

WGROUPS = 2
STEPS = 5
epsilon = 1e-05
highest = lax.Precision.HIGHEST
MESH = pl.DeviceIdType.MESH
F32 = jnp.float32
BF16 = jnp.bfloat16


def fma(a, b):
    return jnp.dot(a, b, preferred_element_type=F32)


def fdot(a, b):
    def halves(m):
        top = m.astype(BF16)
        return top, (m - top.astype(F32)).astype(BF16)

    (a0, a1), (b0, b1) = halves(a), halves(b)
    return fma(jnp.concatenate([a0, a1], axis=1), jnp.concatenate([b0, b0], axis=0)) + fma(a0, b1)


def subsets(stage):
    return [stage] if len(stage) == 1 else [stage[:1], stage[1:], stage]


def main_kernel(
    sizes, stages, parts, whole_count, chunks,
    v_ref, k_ref, hid, white_ref, shift_ref,
    xs, wd, wt, acc, passing, gram, sums, red, got, give, got_pair, fin, got_fin,
    load_sem, send_dir, recv_dir, send_diag, recv_diag, send_pass, recv_pass,
    send_x, recv_x, send_c, recv_c,
    pair_send, pair_recv, tree_send, tree_recv,
):
    nx, ny = sizes
    X, Y, Z, C = v_ref.shape[1:]
    GC = k_ref.shape[1]
    WG = C // WGROUPS
    CH = X // chunks
    me_d = lax.axis_index("dp")
    me_x = lax.axis_index("sx")
    me_y = lax.axis_index("syz")

    def flips(bits):
        where = {}
        for axis, bit in bits:
            me = lax.axis_index(axis)
            where[axis] = where.get(axis, me) + bit - 2 * bit * ((me // bit) % 2)
        return where

    load = pltpu.make_async_copy(
        v_ref.at[0], xs.at[pl.ds(1, X), pl.ds(1, Y), :, pl.ds(C, C)], load_sem)
    load.start()

    odd = me_y % 2
    sign = 2 * odd - 1
    direct, diagonal = me_y - sign, me_y + sign
    behind, ahead = me_y - 2 * sign, me_y + 2 * sign

    def inside(v):
        return (v >= 0) & (v < ny)

    def rerouted(i):
        m = i // 2
        pairs = ny // 2
        return (chunks * jnp.where(i % 2 == 1, pairs - 1 - m, m)) // pairs

    def has_x(d):
        return (me_x + d >= 0) & (me_x + d < nx)

    has_diag = inside(diagonal)
    my_rerouted = jnp.where(has_diag, rerouted(me_y), 0)
    to_pass = jnp.where(inside(behind), rerouted(direct), 0)
    mirrored = (me_x + 1) % 2

    barrier = pltpu.get_barrier_semaphore()

    def greet(where):
        pl.semaphore_signal(barrier, inc=1, device_id=where, device_id_type=MESH)

    pair = flips((("dp", 1),))
    far = [flips(bits) for stage in reversed(stages) for bits in reversed(subsets(stage))] + [pair]
    for who in far:
        greet(who)
    greeted = 0
    other = [(has_x(d) & (me_x % 2 == (0 if d < 0 else 1)), {"sx": me_x + d}) for d in (-1, 1)] if nx > 2 else []
    for ok, where in [
        (has_diag, {"syz": diagonal}),
        (inside(behind), {"syz": behind}),
        (inside(ahead), {"syz": ahead}),
    ] + other:
        @pl.when(ok)
        def _(where=where):
            greet(where)
        greeted += jnp.where(ok, 1, 0)

    lanes = lax.broadcasted_iota(jnp.int32, (GC, C), 1) // GC
    wt[:, :, 0, :, pl.ds(WG, WG)] = jnp.zeros((WGROUPS, 3, 3 * WG, WG), BF16)
    wt[:, :, 3, :, pl.ds(0, WG)] = jnp.zeros((WGROUPS, 3, 3 * WG, WG), BF16)

    @pl.loop(0, k_ref.shape[0])
    def _(t):
        w = k_ref[t].astype(F32)
        for g in range(C // GC):
            masked = jnp.where(lanes == g, w, 0.0).astype(BF16)
            wd[t, pl.ds(g * GC, GC), :] = masked
            h = g * GC // WG
            at = pl.ds(pl.multiple_of((t % 3) * WG + g * GC - h * WG, GC), GC)
            part = masked[:, h * WG:(h + 1) * WG]
            wt[h, t // 9, (t // 3) % 3, at, pl.ds(0, WG)] = part
            wt[h, t // 9, (t // 3) % 3 + 1, at, pl.ds(WG, WG)] = part

    pl.semaphore_wait(barrier, greeted + len(far))

    def plane_of(j):
        return jnp.where(mirrored == 1, X - (j + 1) * CH, j * CH)

    row_direct, row_diag = (Y - 1) * (1 - odd), (Y - 1) * odd
    to_direct, to_diag = (Y + 1) * odd, (Y + 1) * (1 - odd)
    in_direct, in_diag = (Y + 1) * (1 - odd), (Y + 1) * odd

    def middle(px, py):
        return xs.at[px, py, :, pl.ds(C, C)]

    def to_direct_copy(j):
        p = plane_of(j)
        return pltpu.make_async_remote_copy(
            src_ref=v_ref.at[0, pl.ds(p, CH), row_direct],
            dst_ref=middle(pl.ds(p + 1, CH), to_direct),
            send_sem=send_dir.at[j], recv_sem=recv_dir.at[j],
            device_id={"syz": direct}, device_id_type=MESH)

    def to_diag_copy(j):
        p = plane_of(j)
        return pltpu.make_async_remote_copy(
            src_ref=v_ref.at[0, pl.ds(p, CH), row_diag],
            dst_ref=middle(pl.ds(p + 1, CH), to_diag),
            send_sem=send_diag.at[j], recv_sem=recv_diag.at[j],
            device_id={"syz": diagonal}, device_id_type=MESH)

    def detour_copy(j):
        return pltpu.make_async_remote_copy(
            src_ref=v_ref.at[0, pl.ds(plane_of(j), CH), row_diag],
            dst_ref=passing.at[j],
            send_sem=send_diag.at[j], recv_sem=recv_pass.at[j],
            device_id={"syz": direct}, device_id_type=MESH)

    def onward_copy(j):
        return pltpu.make_async_remote_copy(
            src_ref=passing.at[j],
            dst_ref=middle(pl.ds(plane_of(j) + 1, CH), to_direct),
            send_sem=send_pass.at[j], recv_sem=recv_diag.at[j],
            device_id={"syz": behind}, device_id_type=MESH)

    def x_copy(d):
        i = (d + 1) // 2
        return pltpu.make_async_remote_copy(
            src_ref=v_ref.at[0, 0 if d < 0 else X - 1],
            dst_ref=middle(X + 1 if d < 0 else 0, pl.ds(1, Y)),
            send_sem=send_x.at[i], recv_sem=recv_x.at[1 - i],
            device_id={"sx": me_x + d}, device_id_type=MESH)

    def corner_copy(d, side, py):
        i = (d + 1) // 2
        return pltpu.make_async_remote_copy(
            src_ref=middle(1 if d < 0 else X, py),
            dst_ref=middle(X + 1 if d < 0 else 0, py),
            send_sem=send_c.at[i, side], recv_sem=recv_c.at[1 - i, side],
            device_id={"sx": me_x + d}, device_id_type=MESH)

    for j in range(chunks):
        @pl.when(j < my_rerouted)
        def _(j=j):
            detour_copy(j).start()
    for d in (-1, 1):
        @pl.when(has_x(d))
        def _(d=d):
            x_copy(d).start()
    def send(j):
        to_direct_copy(j).start()

        @pl.when(has_diag & (j >= my_rerouted))
        def _():
            to_diag_copy(j).start()

    send(0)

    def pass_on(j):
        @pl.when(j < to_pass)
        def _():
            detour_copy(j).wait_recv()
            onward_copy(j).start()

    rows = lax.broadcasted_iota(jnp.int32, (Z, C), 0)

    def shifted(px, py):
        v = xs[px, py, :, pl.ds(C, C)].astype(F32)
        xs[px, py, :, pl.ds(0, C)] = jnp.where(rows == 0, 0.0, pltpu.roll(v, 1, 0)).astype(BF16)
        xs[px, py, :, pl.ds(2 * C, C)] = jnp.where(
            rows == Z - 1, 0.0, pltpu.roll(v, Z - 1, 0)).astype(BF16)

    load.wait()

    @pl.loop(1, X + 1)
    def _(px):
        for py in range(1, Y + 1):
            shifted(px, py)

    def planes(x, n, offsets, h, fresh):
        for t in range(Y // 2):
            rows = [p for p in range(2 * t - 1, 2 * t + 3) if 0 <= p < Y]
            low = rows[0] - (2 * t - 1)
            def operand(a):
                return [xs[pl.ds(x + 1 + a, n), p + 1, :, pl.ds(c * C + h * WG, WG)].reshape(n * Z, WG)
                        for p in rows for c in range(3)]

            def factor(a):
                return wt[h, a + 1, pl.ds(low, len(rows))].reshape(len(rows) * 3 * WG, 2 * WG)

            both = fma(
                jnp.concatenate([v for a in offsets for v in operand(a)], axis=1),
                jnp.concatenate([factor(a) for a in offsets], axis=0))
            for u in range(2):
                at = (pl.ds(x + 1, n), pl.ds((2 * t + u) * Z, Z), pl.ds(h * WG, WG))
                value = both[:, u * WG:(u + 1) * WG].reshape(n, Z, WG)
                if fresh:
                    acc[at] = value
                else:
                    acc[at] += value

    sides = ((in_direct, True), (in_diag, has_diag))

    def when(ok):
        return (lambda f: f()) if ok is True else pl.when(ok)

    def corners_out(d):
        for side, (py, ok) in enumerate(sides):
            @pl.when(has_x(d) if ok is True else has_x(d) & ok)
            def _(side=side, py=py):
                corner_copy(d, side, py).start()

    def arrived(j):
        to_direct_copy(j).wait_recv()

        @pl.when(has_diag)
        def _():
            to_diag_copy(j).wait_recv()
        for d in (-1, 1):
            if chunks == 1:
                corners_out(d)
            elif j in (0, chunks - 1):
                @pl.when((mirrored == (1 if d > 0 else 0)) == (j == 0))
                def _(d=d):
                    corners_out(d)

    events = ((0, send, 1), (0, send, 2), (0, send, 3), (4, pass_on, 0), (6, pass_on, 1), (6, pass_on, 2), (6, pass_on, 3))
    step = 2 if X % 2 == 0 else 1

    def poll(point):
        for when_at, act, j in events:
            if j < chunks:
                @pl.when(point == when_at)
                def _(act=act, j=j):
                    act(j)

    if X == 1:
        ends = ((0, (0,)),)
    else:
        ends = ((0, (0, 1)), (X - 1, (-1, 0)))
    for h in range(WGROUPS):
        planes(ends[0][0], 1, ends[0][1], h, True)
    if X > 2:
        @pl.loop(0, (X - 2) // step)
        def _(i):
            for h in range(WGROUPS):
                poll(WGROUPS * i + h)
                planes(1 + step * i, step, (-1, 0, 1), h, True)
    for x, offsets in ends[1:]:
        for h in range(WGROUPS):
            planes(x, 1, offsets, h, True)
    reached = WGROUPS * ((X - 2) // step) if X > 2 else 0
    for when_at, act, j in events:
        if j < chunks and when_at >= reached:
            act(j)
    arrived(0)

    for d in (-1, 1):
        @pl.when(has_x(d))
        def _(d=d):
            x_copy(-d).wait_recv()
            px = 0 if d < 0 else X + 1
            for py in range(1, Y + 1):
                shifted(px, py)
            for h in range(WGROUPS):
                planes(0 if d < 0 else X - 1, 1, (d,), h, False)

    def add_row(px0, n, py, x0, a):
        b = jnp.where(py == 0, 0, 2)
        row = pl.ds(pl.multiple_of(jnp.where(py == 0, 0, Y - 1) * Z, Z), Z)
        lhs = xs[pl.ds(px0, n), py].reshape(n * Z, 3 * C)
        w = wd[pl.ds(((a + 1) * 3 + b) * 3, 3)].reshape(3 * C, C)
        acc[pl.ds(x0 + 1, n), row] += fma(lhs, w).reshape(n, Z, C)

    def take(j, p, py):
        for q in range(CH):
            shifted(p + 1 + q, py)
        for a in (-1, 0, 1):
            add_row(p + 1, CH, py, p - a, a)

    def corners_in(d, near):
        here = has_x(d) & ((mirrored == (1 if d > 0 else 0)) == near)
        for side, (py, ok) in enumerate(sides):
            @pl.when(here if ok is True else here & ok)
            def _(side=side, py=py):
                corner_copy(-d, side, py).wait_recv()
                px = 0 if d < 0 else X + 1
                shifted(px, py)
                add_row(px, 1, py, 0 if d < 0 else X - 1, d)

    def add_moments(h):
        for g in range(WGROUPS):
            at = pl.ds(g * WG, WG)
            v = h[:, g * WG:(g + 1) * WG]
            gram[at] += lax.dot_general(v, v, (((0,), (0,)), ((), ())), preferred_element_type=F32)
            sums[:, at] += jnp.sum(v.astype(F32).reshape(-1, 8, WG), axis=0)

    edge_rows = [pl.ds(0, Z), pl.ds((Y - 1) * Z, Z)][:Y]

    def inner_moments(x, n):
        at = pl.ds(Z, (Y - 2) * Z)
        h = acc[pl.ds(x + 1, n), at].astype(BF16)
        hid[pl.ds(x, n), at] = h
        add_moments(h.reshape(-1, C))

    def edge_moments(q, n):
        x = jnp.where(mirrored == 1, X - q - n, q)
        parts = []
        for at in edge_rows:
            h = acc[pl.ds(x + 1, n), at].astype(BF16)
            hid[pl.ds(x, n), at] = h
            parts.append(h.reshape(-1, C))
        add_moments(jnp.concatenate(parts, axis=0))

    gram[...] = jnp.zeros_like(gram)
    sums[...] = jnp.zeros_like(sums)
    if Y > 2:
        group = 4 if X % 4 == 0 else 1

        @pl.loop(0, X // group)
        def _(i):
            inner_moments(group * i, group)
    early = max(0, (chunks - 1) * CH - 1)
    sooner = max(0, (chunks - 2) * CH - 1)
    for j in range(chunks):
        p = plane_of(j)
        if j == chunks - 1:
            if chunks > 1 and not sooner:
                for d in (-1, 1):
                    corners_in(d, True)
            if early:
                edge_moments(sooner, early - sooner)
        if j and j == chunks - 2 and sooner:
            for d in (-1, 1):
                corners_in(d, True)
            edge_moments(0, sooner)
        if j:
            arrived(j)
        for py, ok in sides:
            @when(ok)
            def _(j=j, p=p, py=py):
                take(j, p, py)
    for d in (-1, 1):
        if chunks == 1:
            corners_in(d, True)
        corners_in(d, False)
    edge_moments(early, X - early)

    mine = me_d == 0
    H, Q = WG // 2, WG // 4
    lane_of = lax.broadcasted_iota(jnp.int32, (Q, WG), 1)

    def packed(g):
        row = [gram[pl.ds(g * WG + i * Q, Q)] for i in range(4)]
        mixed = jnp.where(lane_of < Q, pltpu.roll(row[3], Q, 1), row[1])
        folded = jnp.where(lane_of[:Q // 2] < H, pltpu.roll(row[2][:Q // 2], H, 1), row[2][Q // 2:])
        return row[0], mixed, folded, sums[:, pl.ds(g * WG, WG)]

    places = (pl.ds(0, Q), pl.ds(Q, Q), pl.ds(2 * Q, Q // 2), pl.ds(2 * Q + Q // 2, 8))
    low, high = packed(0), packed(1)
    for place, a, b in zip(places, low, high):
        give[place] = jnp.where(mine, b, a)
    swap = pltpu.make_async_remote_copy(
        src_ref=give, dst_ref=got_pair, send_sem=pair_send.at[0], recv_sem=pair_recv.at[0],
        device_id=pair, device_id_type=MESH)
    swap.start()
    for place, a, b in zip(places, low, high):
        red[0, place] = jnp.where(mine, a, b)
    swap.wait()
    red[0] += got_pair[...]

    count = len(stages)

    def legs(step, stream):
        part = pl.ds(*parts[stream])
        return [
            pltpu.make_async_remote_copy(
                src_ref=red.at[step, part], dst_ref=got.at[step, i, part],
                send_sem=tree_send.at[step, stream, i], recv_sem=tree_recv.at[step, stream, i],
                device_id=flips(bits), device_id_type=MESH)
            for i, bits in enumerate(subsets(stages[(step + stream) % count]))]

    def send_sums(step, stream):
        for leg in reversed(legs(step, stream)):
            leg.start()

    for stream in reversed(range(len(parts))):
        send_sums(0, stream)
    for j in range(chunks):
        to_direct_copy(j).wait_send()

        @pl.when(has_diag)
        def _(j=j):
            to_diag_copy(j).wait_send()

        @pl.when(j < to_pass)
        def _(j=j):
            onward_copy(j).wait_send()
    for d in (-1, 1):
        @pl.when(has_x(d))
        def _(d=d):
            x_copy(d).wait_send()
        for side, (py, ok) in enumerate(sides):
            @pl.when(has_x(d) if ok is True else has_x(d) & ok)
            def _(d=d, side=side, py=py):
                corner_copy(d, side, py).wait_send()
    white_ref[...] = jnp.zeros_like(white_ref)
    for step in range(count):
        for stream in range(len(parts)):
            for leg in legs(step, stream):
                leg.wait_recv()
            part = pl.ds(*parts[stream])
            total = red[step, part] + got[step, 0, part]
            if len(stages[(step + stream) % count]) > 1:
                total += got[step, 1, part] + got[step, 2, part]
            red[step + 1, part] = total
            if step + 1 < count:
                send_sums(step + 1, stream)

    average = jnp.sum(red[count, places[3]], axis=0, keepdims=True) / whole_count
    across = jnp.broadcast_to(average, (WG, WG))
    down = across.T
    top, mixed, folded = (red[count, place] for place in places[:3])
    right = jnp.concatenate([top, mixed, pltpu.roll(folded, H, 1), folded, pltpu.roll(mixed, WG - Q, 1)], axis=0)
    column = lax.broadcasted_iota(jnp.int32, (WG, WG), 1) // Q
    moment = jnp.where(column < lax.broadcasted_iota(jnp.int32, (WG, WG), 0) // Q, right.T, right)
    covariance = moment / whole_count - down * across
    identity = jnp.where(
        lax.broadcasted_iota(jnp.int32, (WG, WG), 0) == lax.broadcasted_iota(jnp.int32, (WG, WG), 1),
        1.0, 0.0).astype(F32)
    moved = covariance + epsilon * identity
    square = jnp.sum(jnp.sum(moved * moved, axis=1, keepdims=True), axis=0, keepdims=True)
    frobenius = jnp.sqrt(square)
    y = moved / frobenius
    z = None
    for number in range(STEPS):
        p = 1.5 * identity - 0.5 * (y if z is None else fdot(z, y))
        if number < STEPS - 1:
            y = fdot(y, p)
        z = p if z is None else fdot(p, z)
    whitener = z / jnp.sqrt(frobenius)
    turned = whitener.astype(BF16).astype(F32)
    fin[pl.ds(0, WG)] = turned
    fin[pl.ds(WG, 8)] = jnp.broadcast_to(jnp.sum(turned * down, axis=0, keepdims=True), (8, WG))
    swap = pltpu.make_async_remote_copy(
        src_ref=fin, dst_ref=got_fin, send_sem=pair_send.at[1], recv_sem=pair_recv.at[1],
        device_id=pair, device_id_type=MESH)
    swap.start()
    own = fin[...]
    for step in range(count):
        for stream in range(len(parts)):
            for leg in legs(step, stream):
                leg.wait_send()
    swap.wait()
    other = got_fin[...]
    first = jnp.where(mine, own, other)
    second = jnp.where(mine, other, own)
    white_ref[pl.ds(0, WG), pl.ds(0, WG)] = first[:WG].astype(BF16)
    white_ref[pl.ds(WG, WG), pl.ds(WG, WG)] = second[:WG].astype(BF16)
    shift_ref[:, pl.ds(0, WG)] = first[WG:]
    shift_ref[:, pl.ds(WG, WG)] = second[WG:]


def apply_kernel(h_ref, w_ref, s_ref, o_ref, block, sems):
    X, Y = block.shape[:2]
    M = h_ref.shape[1] // 2
    copies = []
    for x in range(X):
        for half in range(2):
            rows = pl.ds(half * (Y // 2), Y // 2)
            result = fma(h_ref[x, pl.ds(half * M, M)], w_ref[...]) - s_ref[0:1, :]
            block[x, rows] = result.astype(BF16).reshape(Y // 2, *block.shape[2:])
            copies.append(pltpu.make_async_copy(block.at[x, rows], o_ref.at[x, rows], sems.at[x, half]))
            copies[-1].start()
    for copy in copies:
        copy.wait()


def on_device(sizes, volume, kernel):
    nd, nx, ny = sizes
    X, Y, Z, C = volume.shape[1:]
    GC = kernel.shape[3]
    WG = C // WGROUPS
    stages = []
    for axis, n in (("sx", nx), ("syz", ny)):
        bit = 1
        while bit < n:
            stages.append((axis, bit))
            bit *= 2
    stages = [tuple(stages[i:i + 2]) for i in range(0, len(stages), 2)]
    streams = len(stages)
    R = 5 * WG // 8 + 8
    blocks = R // 8
    edges = [8 * (blocks * i // streams) for i in range(streams + 1)]
    parts = [(edges[i], edges[i + 1] - edges[i]) for i in range(streams)]
    whole_count = float(X * Y * Z * nd * nx * ny)
    count = len(stages)
    dma = pltpu.SemaphoreType.DMA
    chunks = max(n for n in (1, 2, 4) if X % n == 0)
    hidden, white, shift = pl.pallas_call(
        functools.partial(main_kernel, (nx, ny), tuple(stages), tuple(parts), whole_count, chunks),
        out_shape=(
            pltpu.VMEM((X, Y * Z, C), BF16),
            pltpu.VMEM((C, C), BF16),
            pltpu.VMEM((8, C), F32),
        ),
        in_specs=[pl.BlockSpec(memory_space=pl.ANY), pl.BlockSpec(memory_space=pltpu.VMEM)],
        out_specs=(
            pl.BlockSpec(memory_space=pltpu.VMEM),
            pl.BlockSpec(memory_space=pltpu.VMEM),
            pl.BlockSpec(memory_space=pltpu.VMEM),
        ),
        scratch_shapes=[
            pltpu.VMEM((X + 2, Y + 2, Z, 3 * C), BF16),
            pltpu.VMEM((27, C, C), BF16),
            pltpu.VMEM((WGROUPS, 3, 4, 3 * WG, 2 * WG), BF16),
            pltpu.VMEM((X + 2, Y * Z, C), F32),
            pltpu.VMEM((chunks, X // chunks, Z, C), BF16),
            pltpu.VMEM((C, WG), F32),
            pltpu.VMEM((8, C), F32),
            pltpu.VMEM((count + 1, R, WG), F32),
            pltpu.VMEM((count, 3, R, WG), F32),
            pltpu.VMEM((R, WG), F32),
            pltpu.VMEM((R, WG), F32),
            pltpu.VMEM((WG + 8, WG), F32),
            pltpu.VMEM((WG + 8, WG), F32),
            dma, dma((chunks,)), dma((chunks,)), dma((chunks,)), dma((chunks,)), dma((chunks,)), dma((chunks,)),
            dma((2,)), dma((2,)), dma((2, 2)), dma((2, 2)),
            dma((2,)), dma((2,)), dma((count, streams, 3)), dma((count, streams, 3)),
        ],
        compiler_params=pltpu.CompilerParams(
            collective_id=0, has_side_effects=True, vmem_limit_bytes=56 * 2**20),
        name="conv_moments",
    )(volume, kernel.reshape(27, GC, C))
    result = pl.pallas_call(
        apply_kernel,
        out_shape=jax.ShapeDtypeStruct((X, Y, Z, C), BF16),
        in_specs=[pl.BlockSpec(memory_space=pltpu.VMEM)] * 3,
        out_specs=pl.BlockSpec(memory_space=pl.ANY),
        scratch_shapes=[pltpu.VMEM((X, Y, Z, C), BF16), dma((X, 2))],
        name="apply",
    )(*(pltpu.with_memory_space_constraint(v, pltpu.VMEM) for v in (hidden, white, shift)))
    return result.reshape(volume.shape)


def solution(mesh):
    sizes = (mesh.shape["dp"], mesh.shape["sx"], mesh.shape["syz"])
    placed = (P("dp", "sx", "syz", None, None), P())
    return jax.shard_map(
        functools.partial(on_device, sizes),
        mesh=mesh,
        in_specs=placed,
        out_specs=P("dp", "sx", "syz", None, None),
        check_vma=False,
    )
```

```python
import functools

import jax
import jax.numpy as jnp
from jax import lax
from jax.experimental import pallas as pl
from jax.experimental.pallas import tpu as pltpu
from jax.sharding import PartitionSpec as P

WGROUPS = 2
STEPS = 5
epsilon = 1e-05
highest = lax.Precision.HIGHEST
MESH = pl.DeviceIdType.MESH
F32 = jnp.float32
BF16 = jnp.bfloat16


def fma(a, b):
    return jnp.dot(a, b, preferred_element_type=F32)


def fdot(a, b):
    def halves(m):
        top = m.astype(BF16)
        return top, (m - top.astype(F32)).astype(BF16)

    n = b.shape[1]
    left = jnp.concatenate(halves(a), axis=1)
    right = jnp.concatenate(halves(b), axis=1)
    both = fma(left, jnp.concatenate([right, right], axis=0))
    return both[:, :n] + both[:, n:]


def subsets(stage):
    return [stage] if len(stage) == 1 else [stage[:1], stage[1:], stage]


def main_kernel(
    sizes, stages, parts, whole_count, chunks,
    v_ref, k_ref, hid, white_ref, shift_ref,
    xs, wd, wt, acc, passing, gram, sums, red, got, give, got_pair, fin, got_fin,
    load_sem, send_dir, recv_dir, send_diag, recv_diag, send_pass, recv_pass,
    send_x, recv_x, send_c, recv_c,
    pair_send, pair_recv, tree_send, tree_recv,
):
    nx, ny = sizes
    X, Y, Z, C = v_ref.shape[1:]
    GC = k_ref.shape[1]
    WG = C // WGROUPS
    CH = X // chunks
    me_d = lax.axis_index("dp")
    me_x = lax.axis_index("sx")
    me_y = lax.axis_index("syz")

    def flips(bits):
        where = {}
        for axis, bit in bits:
            me = lax.axis_index(axis)
            where[axis] = where.get(axis, me) + bit - 2 * bit * ((me // bit) % 2)
        return where

    load = pltpu.make_async_copy(
        v_ref.at[0], xs.at[pl.ds(1, X), pl.ds(1, Y), :, pl.ds(C, C)], load_sem)
    load.start()

    odd = me_y % 2
    sign = 2 * odd - 1
    direct, diagonal = me_y - sign, me_y + sign
    behind, ahead = me_y - 2 * sign, me_y + 2 * sign

    def inside(v):
        return (v >= 0) & (v < ny)

    def rerouted(i):
        m = i // 2
        pairs = ny // 2
        return (chunks * jnp.where(i % 2 == 1, pairs - 1 - m, m)) // pairs

    def has_x(d):
        return (me_x + d >= 0) & (me_x + d < nx)

    has_diag = inside(diagonal)
    my_rerouted = jnp.where(has_diag, rerouted(me_y), 0)
    to_pass = jnp.where(inside(behind), rerouted(direct), 0)
    mirrored = (me_x + 1) % 2

    barrier = pltpu.get_barrier_semaphore()

    def greet(where):
        pl.semaphore_signal(barrier, inc=1, device_id=where, device_id_type=MESH)

    pair = flips((("dp", 1),))
    far = [flips(bits) for stage in reversed(stages) for bits in reversed(subsets(stage))] + [pair]
    for who in far:
        greet(who)
    greeted = 0
    other = [(has_x(d) & (me_x % 2 == (0 if d < 0 else 1)), {"sx": me_x + d}) for d in (-1, 1)] if nx > 2 else []
    for ok, where in [
        (has_diag, {"syz": diagonal}),
        (inside(behind), {"syz": behind}),
        (inside(ahead), {"syz": ahead}),
    ] + other:
        @pl.when(ok)
        def _(where=where):
            greet(where)
        greeted += jnp.where(ok, 1, 0)

    lanes = lax.broadcasted_iota(jnp.int32, (GC, C), 1) // GC
    wt[:, :, 0, :, pl.ds(WG, WG)] = jnp.zeros((WGROUPS, 3, 3 * WG, WG), BF16)
    wt[:, :, 3, :, pl.ds(0, WG)] = jnp.zeros((WGROUPS, 3, 3 * WG, WG), BF16)

    @pl.loop(0, k_ref.shape[0])
    def _(t):
        w = k_ref[t].astype(F32)
        for g in range(C // GC):
            masked = jnp.where(lanes == g, w, 0.0).astype(BF16)
            wd[t, pl.ds(g * GC, GC), :] = masked
            h = g * GC // WG
            at = pl.ds(pl.multiple_of((t % 3) * WG + g * GC - h * WG, GC), GC)
            part = masked[:, h * WG:(h + 1) * WG]
            wt[h, t // 9, (t // 3) % 3, at, pl.ds(0, WG)] = part
            wt[h, t // 9, (t // 3) % 3 + 1, at, pl.ds(WG, WG)] = part

    pl.semaphore_wait(barrier, greeted + len(far))

    def plane_of(j):
        return jnp.where(mirrored == 1, X - (j + 1) * CH, j * CH)

    row_direct, row_diag = (Y - 1) * (1 - odd), (Y - 1) * odd
    to_direct, to_diag = (Y + 1) * odd, (Y + 1) * (1 - odd)
    in_direct, in_diag = (Y + 1) * (1 - odd), (Y + 1) * odd

    def middle(px, py):
        return xs.at[px, py, :, pl.ds(C, C)]

    def to_direct_copy(j):
        p = plane_of(j)
        return pltpu.make_async_remote_copy(
            src_ref=v_ref.at[0, pl.ds(p, CH), row_direct],
            dst_ref=middle(pl.ds(p + 1, CH), to_direct),
            send_sem=send_dir.at[j], recv_sem=recv_dir.at[j],
            device_id={"syz": direct}, device_id_type=MESH)

    def to_diag_copy(j):
        p = plane_of(j)
        return pltpu.make_async_remote_copy(
            src_ref=v_ref.at[0, pl.ds(p, CH), row_diag],
            dst_ref=middle(pl.ds(p + 1, CH), to_diag),
            send_sem=send_diag.at[j], recv_sem=recv_diag.at[j],
            device_id={"syz": diagonal}, device_id_type=MESH)

    def detour_copy(j):
        return pltpu.make_async_remote_copy(
            src_ref=v_ref.at[0, pl.ds(plane_of(j), CH), row_diag],
            dst_ref=passing.at[j],
            send_sem=send_diag.at[j], recv_sem=recv_pass.at[j],
            device_id={"syz": direct}, device_id_type=MESH)

    def onward_copy(j):
        return pltpu.make_async_remote_copy(
            src_ref=passing.at[j],
            dst_ref=middle(pl.ds(plane_of(j) + 1, CH), to_direct),
            send_sem=send_pass.at[j], recv_sem=recv_diag.at[j],
            device_id={"syz": behind}, device_id_type=MESH)

    def x_copy(d):
        i = (d + 1) // 2
        return pltpu.make_async_remote_copy(
            src_ref=v_ref.at[0, 0 if d < 0 else X - 1],
            dst_ref=middle(X + 1 if d < 0 else 0, pl.ds(1, Y)),
            send_sem=send_x.at[i], recv_sem=recv_x.at[1 - i],
            device_id={"sx": me_x + d}, device_id_type=MESH)

    def corner_copy(d, side, py):
        i = (d + 1) // 2
        return pltpu.make_async_remote_copy(
            src_ref=middle(1 if d < 0 else X, py),
            dst_ref=middle(X + 1 if d < 0 else 0, py),
            send_sem=send_c.at[i, side], recv_sem=recv_c.at[1 - i, side],
            device_id={"sx": me_x + d}, device_id_type=MESH)

    for j in range(chunks):
        @pl.when(j < my_rerouted)
        def _(j=j):
            detour_copy(j).start()
    for d in (-1, 1):
        @pl.when(has_x(d))
        def _(d=d):
            x_copy(d).start()
    def send(j):
        to_direct_copy(j).start()

        @pl.when(has_diag & (j >= my_rerouted))
        def _():
            to_diag_copy(j).start()

    send(0)

    def pass_on(j):
        @pl.when(j < to_pass)
        def _():
            detour_copy(j).wait_recv()
            onward_copy(j).start()

    rows = lax.broadcasted_iota(jnp.int32, (Z, C), 0)

    def shifted(px, py):
        v = xs[px, py, :, pl.ds(C, C)].astype(F32)
        xs[px, py, :, pl.ds(0, C)] = jnp.where(rows == 0, 0.0, pltpu.roll(v, 1, 0)).astype(BF16)
        xs[px, py, :, pl.ds(2 * C, C)] = jnp.where(
            rows == Z - 1, 0.0, pltpu.roll(v, Z - 1, 0)).astype(BF16)

    load.wait()

    @pl.loop(1, X + 1)
    def _(px):
        for py in range(1, Y + 1):
            shifted(px, py)

    def planes(x, n, offsets, h, fresh):
        for t in range(Y // 2):
            rows = [p for p in range(2 * t - 1, 2 * t + 3) if 0 <= p < Y]
            low = rows[0] - (2 * t - 1)
            def operand(a):
                return [xs[pl.ds(x + 1 + a, n), p + 1, :, pl.ds(c * C + h * WG, WG)].reshape(n * Z, WG)
                        for p in rows for c in range(3)]

            def factor(a):
                return wt[h, a + 1, pl.ds(low, len(rows))].reshape(len(rows) * 3 * WG, 2 * WG)

            both = fma(
                jnp.concatenate([v for a in offsets for v in operand(a)], axis=1),
                jnp.concatenate([factor(a) for a in offsets], axis=0))
            for u in range(2):
                at = (pl.ds(x + 1, n), pl.ds((2 * t + u) * Z, Z), pl.ds(h * WG, WG))
                value = both[:, u * WG:(u + 1) * WG].reshape(n, Z, WG)
                if fresh:
                    acc[at] = value
                else:
                    acc[at] += value

    sides = ((in_direct, True), (in_diag, has_diag))

    def when(ok):
        return (lambda f: f()) if ok is True else pl.when(ok)

    def corners_out(d):
        for side, (py, ok) in enumerate(sides):
            @pl.when(has_x(d) if ok is True else has_x(d) & ok)
            def _(side=side, py=py):
                corner_copy(d, side, py).start()

    def arrived(j):
        to_direct_copy(j).wait_recv()

        @pl.when(has_diag)
        def _():
            to_diag_copy(j).wait_recv()
        for d in (-1, 1):
            if chunks == 1:
                corners_out(d)
            elif j in (0, chunks - 1):
                @pl.when((mirrored == (1 if d > 0 else 0)) == (j == 0))
                def _(d=d):
                    corners_out(d)

    events = ((0, send, 1), (0, send, 2), (0, send, 3), (4, pass_on, 0), (6, pass_on, 1), (6, pass_on, 2), (6, pass_on, 3))
    step = 2 if X % 2 == 0 else 1

    def poll(point):
        for when_at, act, j in events:
            if j < chunks:
                @pl.when(point == when_at)
                def _(act=act, j=j):
                    act(j)

    if X == 1:
        ends = ((0, (0,)),)
    else:
        ends = ((0, (0, 1)), (X - 1, (-1, 0)))
    for h in range(WGROUPS):
        planes(ends[0][0], 1, ends[0][1], h, True)
    if X > 2:
        @pl.loop(0, (X - 2) // step)
        def _(i):
            for h in range(WGROUPS):
                poll(WGROUPS * i + h)
                planes(1 + step * i, step, (-1, 0, 1), h, True)
    for x, offsets in ends[1:]:
        for h in range(WGROUPS):
            planes(x, 1, offsets, h, True)
    reached = WGROUPS * ((X - 2) // step) if X > 2 else 0
    for when_at, act, j in events:
        if j < chunks and when_at >= reached:
            act(j)
    arrived(0)

    for d in (-1, 1):
        @pl.when(has_x(d))
        def _(d=d):
            x_copy(-d).wait_recv()
            px = 0 if d < 0 else X + 1
            for py in range(1, Y + 1):
                shifted(px, py)
            for h in range(WGROUPS):
                planes(0 if d < 0 else X - 1, 1, (d,), h, False)

    def add_row(px0, n, py, x0, a):
        b = jnp.where(py == 0, 0, 2)
        row = pl.ds(pl.multiple_of(jnp.where(py == 0, 0, Y - 1) * Z, Z), Z)
        lhs = xs[pl.ds(px0, n), py].reshape(n * Z, 3 * C)
        w = wd[pl.ds(((a + 1) * 3 + b) * 3, 3)].reshape(3 * C, C)
        acc[pl.ds(x0 + 1, n), row] += fma(lhs, w).reshape(n, Z, C)

    def take(j, p, py):
        for q in range(CH):
            shifted(p + 1 + q, py)
        for a in (-1, 0, 1):
            add_row(p + 1, CH, py, p - a, a)

    def corners_in(d, near):
        here = has_x(d) & ((mirrored == (1 if d > 0 else 0)) == near)
        for side, (py, ok) in enumerate(sides):
            @pl.when(here if ok is True else here & ok)
            def _(side=side, py=py):
                corner_copy(-d, side, py).wait_recv()
                px = 0 if d < 0 else X + 1
                shifted(px, py)
                add_row(px, 1, py, 0 if d < 0 else X - 1, d)

    def add_moments(h):
        for g in range(WGROUPS):
            at = pl.ds(g * WG, WG)
            v = h[:, g * WG:(g + 1) * WG]
            gram[at] += lax.dot_general(v, v, (((0,), (0,)), ((), ())), preferred_element_type=F32)
            sums[:, at] += jnp.sum(v.astype(F32).reshape(-1, 8, WG), axis=0)

    edge_rows = [pl.ds(0, Z), pl.ds((Y - 1) * Z, Z)][:Y]

    def inner_moments(x, n):
        at = pl.ds(Z, (Y - 2) * Z)
        h = acc[pl.ds(x + 1, n), at].astype(BF16)
        hid[pl.ds(x, n), at] = h
        add_moments(h.reshape(-1, C))

    def edge_moments(q, n):
        x = jnp.where(mirrored == 1, X - q - n, q)
        parts = []
        for at in edge_rows:
            h = acc[pl.ds(x + 1, n), at].astype(BF16)
            hid[pl.ds(x, n), at] = h
            parts.append(h.reshape(-1, C))
        add_moments(jnp.concatenate(parts, axis=0))

    gram[...] = jnp.zeros_like(gram)
    sums[...] = jnp.zeros_like(sums)
    if Y > 2:
        group = 4 if X % 4 == 0 else 1

        @pl.loop(0, X // group)
        def _(i):
            inner_moments(group * i, group)
    early = max(0, (chunks - 1) * CH - 1)
    sooner = max(0, (chunks - 2) * CH - 1)
    for j in range(chunks):
        p = plane_of(j)
        if j == chunks - 1:
            if chunks > 1 and not sooner:
                for d in (-1, 1):
                    corners_in(d, True)
            if early:
                edge_moments(sooner, early - sooner)
        if j and j == chunks - 2 and sooner:
            for d in (-1, 1):
                corners_in(d, True)
            edge_moments(0, sooner)
        if j:
            arrived(j)
        for py, ok in sides:
            @when(ok)
            def _(j=j, p=p, py=py):
                take(j, p, py)
    for d in (-1, 1):
        if chunks == 1:
            corners_in(d, True)
        corners_in(d, False)
    edge_moments(early, X - early)

    mine = me_d == 0
    H, Q = WG // 2, WG // 4
    lane_of = lax.broadcasted_iota(jnp.int32, (Q, WG), 1)

    def packed(g):
        row = [gram[pl.ds(g * WG + i * Q, Q)] for i in range(4)]
        mixed = jnp.where(lane_of < Q, pltpu.roll(row[3], Q, 1), row[1])
        folded = jnp.where(lane_of[:Q // 2] < H, pltpu.roll(row[2][:Q // 2], H, 1), row[2][Q // 2:])
        return row[0], mixed, folded, sums[:, pl.ds(g * WG, WG)]

    places = (pl.ds(0, Q), pl.ds(Q, Q), pl.ds(2 * Q, Q // 2), pl.ds(2 * Q + Q // 2, 8))
    low, high = packed(0), packed(1)
    for place, a, b in zip(places, low, high):
        give[place] = jnp.where(mine, b, a)
    swap = pltpu.make_async_remote_copy(
        src_ref=give, dst_ref=got_pair, send_sem=pair_send.at[0], recv_sem=pair_recv.at[0],
        device_id=pair, device_id_type=MESH)
    swap.start()
    for place, a, b in zip(places, low, high):
        red[0, place] = jnp.where(mine, a, b)
    swap.wait()
    red[0] += got_pair[...]

    count = len(stages)

    def legs(step, stream):
        part = pl.ds(*parts[stream])
        return [
            pltpu.make_async_remote_copy(
                src_ref=red.at[step, part], dst_ref=got.at[step, i, part],
                send_sem=tree_send.at[step, stream, i], recv_sem=tree_recv.at[step, stream, i],
                device_id=flips(bits), device_id_type=MESH)
            for i, bits in enumerate(subsets(stages[(step + stream) % count]))]

    def send_sums(step, stream):
        for leg in reversed(legs(step, stream)):
            leg.start()

    for stream in reversed(range(len(parts))):
        send_sums(0, stream)
    for j in range(chunks):
        to_direct_copy(j).wait_send()

        @pl.when(has_diag)
        def _(j=j):
            to_diag_copy(j).wait_send()

        @pl.when(j < to_pass)
        def _(j=j):
            onward_copy(j).wait_send()
    for d in (-1, 1):
        @pl.when(has_x(d))
        def _(d=d):
            x_copy(d).wait_send()
        for side, (py, ok) in enumerate(sides):
            @pl.when(has_x(d) if ok is True else has_x(d) & ok)
            def _(d=d, side=side, py=py):
                corner_copy(d, side, py).wait_send()
    white_ref[...] = jnp.zeros_like(white_ref)
    for step in range(count):
        for stream in range(len(parts)):
            for leg in legs(step, stream):
                leg.wait_recv()
            part = pl.ds(*parts[stream])
            total = red[step, part] + got[step, 0, part]
            if len(stages[(step + stream) % count]) > 1:
                total += got[step, 1, part] + got[step, 2, part]
            red[step + 1, part] = total
            if step + 1 < count:
                send_sums(step + 1, stream)

    average = jnp.sum(red[count, places[3]], axis=0, keepdims=True) / whole_count
    across = jnp.broadcast_to(average, (WG, WG))
    down = across.T
    top, mixed, folded = (red[count, place] for place in places[:3])
    right = jnp.concatenate([top, mixed, pltpu.roll(folded, H, 1), folded, pltpu.roll(mixed, WG - Q, 1)], axis=0)
    column = lax.broadcasted_iota(jnp.int32, (WG, WG), 1) // Q
    moment = jnp.where(column < lax.broadcasted_iota(jnp.int32, (WG, WG), 0) // Q, right.T, right)
    covariance = moment / whole_count - down * across
    identity = jnp.where(
        lax.broadcasted_iota(jnp.int32, (WG, WG), 0) == lax.broadcasted_iota(jnp.int32, (WG, WG), 1),
        1.0, 0.0).astype(F32)
    moved = covariance + epsilon * identity
    square = jnp.sum(jnp.sum(moved * moved, axis=1, keepdims=True), axis=0, keepdims=True)
    frobenius = jnp.sqrt(square)
    y = moved / frobenius
    z = None
    for number in range(STEPS):
        p = 1.5 * identity - 0.5 * (y if z is None else fdot(z, y))
        if number < STEPS - 1:
            y = fdot(y, p)
        z = p if z is None else fdot(p, z)
    whitener = z / jnp.sqrt(frobenius)
    turned = whitener.astype(BF16).astype(F32)
    fin[pl.ds(0, WG)] = turned
    fin[pl.ds(WG, 8)] = jnp.broadcast_to(jnp.sum(turned * down, axis=0, keepdims=True), (8, WG))
    swap = pltpu.make_async_remote_copy(
        src_ref=fin, dst_ref=got_fin, send_sem=pair_send.at[1], recv_sem=pair_recv.at[1],
        device_id=pair, device_id_type=MESH)
    swap.start()
    own = fin[...]
    for step in range(count):
        for stream in range(len(parts)):
            for leg in legs(step, stream):
                leg.wait_send()
    swap.wait()
    other = got_fin[...]
    first = jnp.where(mine, own, other)
    second = jnp.where(mine, other, own)
    white_ref[pl.ds(0, WG), pl.ds(0, WG)] = first[:WG].astype(BF16)
    white_ref[pl.ds(WG, WG), pl.ds(WG, WG)] = second[:WG].astype(BF16)
    shift_ref[:, pl.ds(0, WG)] = first[WG:]
    shift_ref[:, pl.ds(WG, WG)] = second[WG:]


def apply_kernel(h_ref, w_ref, s_ref, o_ref, block, sems):
    X, Y = block.shape[:2]
    M = h_ref.shape[1] // 2
    copies = []
    for x in range(X):
        for half in range(2):
            rows = pl.ds(half * (Y // 2), Y // 2)
            result = fma(h_ref[x, pl.ds(half * M, M)], w_ref[...]) - s_ref[0:1, :]
            block[x, rows] = result.astype(BF16).reshape(Y // 2, *block.shape[2:])
            copies.append(pltpu.make_async_copy(block.at[x, rows], o_ref.at[x, rows], sems.at[x, half]))
            copies[-1].start()
    for copy in copies:
        copy.wait()


def on_device(sizes, volume, kernel):
    nd, nx, ny = sizes
    X, Y, Z, C = volume.shape[1:]
    GC = kernel.shape[3]
    WG = C // WGROUPS
    stages = []
    for axis, n in (("sx", nx), ("syz", ny)):
        bit = 1
        while bit < n:
            stages.append((axis, bit))
            bit *= 2
    stages = [tuple(stages[i:i + 2]) for i in range(0, len(stages), 2)]
    streams = len(stages)
    R = 5 * WG // 8 + 8
    blocks = R // 8
    edges = [8 * (blocks * i // streams) for i in range(streams + 1)]
    parts = [(edges[i], edges[i + 1] - edges[i]) for i in range(streams)]
    whole_count = float(X * Y * Z * nd * nx * ny)
    count = len(stages)
    dma = pltpu.SemaphoreType.DMA
    chunks = max(n for n in (1, 2, 4) if X % n == 0)
    hidden, white, shift = pl.pallas_call(
        functools.partial(main_kernel, (nx, ny), tuple(stages), tuple(parts), whole_count, chunks),
        out_shape=(
            pltpu.VMEM((X, Y * Z, C), BF16),
            pltpu.VMEM((C, C), BF16),
            pltpu.VMEM((8, C), F32),
        ),
        in_specs=[pl.BlockSpec(memory_space=pl.ANY), pl.BlockSpec(memory_space=pltpu.VMEM)],
        out_specs=(
            pl.BlockSpec(memory_space=pltpu.VMEM),
            pl.BlockSpec(memory_space=pltpu.VMEM),
            pl.BlockSpec(memory_space=pltpu.VMEM),
        ),
        scratch_shapes=[
            pltpu.VMEM((X + 2, Y + 2, Z, 3 * C), BF16),
            pltpu.VMEM((27, C, C), BF16),
            pltpu.VMEM((WGROUPS, 3, 4, 3 * WG, 2 * WG), BF16),
            pltpu.VMEM((X + 2, Y * Z, C), F32),
            pltpu.VMEM((chunks, X // chunks, Z, C), BF16),
            pltpu.VMEM((C, WG), F32),
            pltpu.VMEM((8, C), F32),
            pltpu.VMEM((count + 1, R, WG), F32),
            pltpu.VMEM((count, 3, R, WG), F32),
            pltpu.VMEM((R, WG), F32),
            pltpu.VMEM((R, WG), F32),
            pltpu.VMEM((WG + 8, WG), F32),
            pltpu.VMEM((WG + 8, WG), F32),
            dma, dma((chunks,)), dma((chunks,)), dma((chunks,)), dma((chunks,)), dma((chunks,)), dma((chunks,)),
            dma((2,)), dma((2,)), dma((2, 2)), dma((2, 2)),
            dma((2,)), dma((2,)), dma((count, streams, 3)), dma((count, streams, 3)),
        ],
        compiler_params=pltpu.CompilerParams(
            collective_id=0, has_side_effects=True, vmem_limit_bytes=56 * 2**20),
        name="conv_moments",
    )(volume, kernel.reshape(27, GC, C))
    result = pl.pallas_call(
        apply_kernel,
        out_shape=jax.ShapeDtypeStruct((X, Y, Z, C), BF16),
        in_specs=[pl.BlockSpec(memory_space=pltpu.VMEM)] * 3,
        out_specs=pl.BlockSpec(memory_space=pl.ANY),
        scratch_shapes=[pltpu.VMEM((X, Y, Z, C), BF16), dma((X, 2))],
        name="apply",
    )(*(pltpu.with_memory_space_constraint(v, pltpu.VMEM) for v in (hidden, white, shift)))
    return result.reshape(volume.shape)


def solution(mesh):
    sizes = (mesh.shape["dp"], mesh.shape["sx"], mesh.shape["syz"])
    placed = (P("dp", "sx", "syz", None, None), P())
    return jax.shard_map(
        functools.partial(on_device, sizes),
        mesh=mesh,
        in_specs=placed,
        out_specs=P("dp", "sx", "syz", None, None),
        check_vma=False,
    )
```
